32 devices in a mesh: dp: 16 (over z, y, core), tensor: 2 (over x).
Axes of the slice: x: 2, y: 2, z: 4, core: 2. Of those that a mesh axis runs over, the one named last changes fastest.
Arguments:
- residual: float32 [4096, 1024], P(('dp', 'tensor')), may hold values from -6 to 6
- segment_ids: int32 [4096], P('dp'), may hold values from 0 to 3, as said below
- live_counts: int32 [16], P('dp'), may hold values from 128 to 256, as said below
- norm_gain: float32 [1024], replicated, may hold values from 0.5 to 1.5
- z_weight: bfloat16 [1024, 2048], P('dp', 'tensor'), may hold values from -0.1875 to 0.1875
- x_weight: bfloat16 [1024, 2048], P('dp', 'tensor'), may hold values from -0.1875 to 0.1875
- bc_weight: bfloat16 [1024, 256], P('dp'), may hold values from -0.1875 to 0.1875
- dt_weight: bfloat16 [1024, 32], P('dp', 'tensor'), may hold values from -0.1875 to 0.1875
- conv_x: float32 [4, 2048], P(None, 'tensor'), may hold values from -3 to 3
- conv_x_bias: float32 [2048], P('tensor'), may hold values from -3 to 3
- conv_bc: float32 [4, 256], replicated, may hold values from -3 to 3
- conv_bc_bias: float32 [256], replicated, may hold values from -3 to 3
- dt_bias: float32 [32], P('tensor'), may hold values from -6.9 to -2.3
- a_log: float32 [32], P('tensor'), may hold values from 0 to 2.77
- d_skip: float32 [32], P('tensor'), may hold values from 0.5 to 1.5
- gate_gain: float32 [2048], P('tensor'), may hold values from 0.5 to 1.5
- out_weight: bfloat16 [2048, 1024], P('tensor', 'dp'), may hold values from -0.125 to 0.125
- cotangent: float32 [4096, 1024], P(('dp', 'tensor')), may hold values from -6 to 6
Outputs:
- block_out: float32 [4096, 1024], P(('dp', 'tensor'))
- input_grad: float32 [4096, 1024], P(('dp', 'tensor'))
- norm_gain_grad: float32 [1024], replicated
- z_weight_grad: float32 [1024, 2048], P('dp', 'tensor')
- x_weight_grad: float32 [1024, 2048], P('dp', 'tensor')
- bc_weight_grad: float32 [1024, 256], P(('dp', 'tensor'))
- dt_weight_grad: float32 [1024, 32], P('dp', 'tensor')
- conv_x_grad: float32 [4, 2048], P(None, 'tensor')
- conv_x_bias_grad: float32 [2048], P('tensor')
- conv_bc_grad: float32 [4, 256], replicated
- conv_bc_bias_grad: float32 [256], replicated
- dt_bias_grad: float32 [32], P('tensor')
- a_log_grad: float32 [32], P('tensor')
- d_skip_grad: float32 [32], P('tensor')
- gate_gain_grad: float32 [2048], P('tensor')
- out_weight_grad: float32 [2048, 1024], P('tensor', 'dp')
The draws below stay inside these ranges and needn't reach their ends.
Inputs may be any that keep to these rules, and one draw needn't show every extreme that they name: `segment_ids`: Non-decreasing along each stream of 256 slots, starting at 0, rising by one at exactly three slots of every stream. `live_counts`: one stream is full and one holds exactly half.
All inputs are finite; a program needn't handle non-finite values.
Results may differ from the reference program's by a relative error of at most 0.0082.
Values may be sent and summed in bfloat16 or wider, within the bound.
No kernel may reach another device: no remote copies, remote signals or barrier semaphores. Data moves between devices by JAX's collectives and lax.ppermute only.
A program may use at most 128 MiB of HBM per device.

```python
from functools import partial
import jax
import jax.numpy as jnp
from jax import lax

D = 1024
HEADS = 32
STATE = 128
CONV = 4
SPAN = 128
TOK_DEV = 256
INNER = 2048
STREAMS = 16
TOKENS = 4096
N_TENSOR = 2


def stream_ids(key):
    order = jax.random.permutation(key, TOK_DEV - 1) + 1
    cut_points = order[:3]
    slots = jnp.arange(TOK_DEV)
    return jnp.sum((cut_points[None, :] <= slots[:, None]).astype(jnp.int32), axis=1).astype(jnp.int32)


def draw_segment_ids(key, part):
    keys = jax.random.split(key, STREAMS)
    return jax.vmap(stream_ids)(keys).reshape(STREAMS * TOK_DEV).astype(jnp.int32)


def draw_live_counts(key, part):
    values = jax.random.randint(key, (STREAMS,), TOK_DEV // 2, TOK_DEV + 1)
    full_index = jax.random.randint(jax.random.fold_in(key, 1), (), 0, STREAMS)
    other_index = (full_index + 1 + jax.random.randint(jax.random.fold_in(key, 2), (), 0, STREAMS - 1)) % STREAMS
    indices = jnp.arange(STREAMS)
    values = jnp.where(indices == full_index, TOK_DEV, values)
    values = jnp.where(indices == other_index, TOK_DEV // 2, values)
    return values.astype(jnp.int32)


def spiked(values, own_key, source, target, blocks, factor):
    owner, partner = [(jnp.arange(values.shape[position]) // (values.shape[position] // blocks)).reshape([-1 if axis == position else 1 for axis in range(values.ndim)]) for position in (source, target)]
    chosen = jax.random.permutation(own_key, blocks)[partner]
    strong = (owner == chosen) | (owner == (partner + blocks // 2) % blocks)
    return jnp.where(strong, factor * values, values)


def steps_of(key, shape, cuts, low, largest):
    loudness = 1.0
    for axis_at, shards_of in cuts:
        draws = jax.random.uniform(jax.random.fold_in(jax.random.fold_in(key, 6), axis_at), (shards_of,), jnp.float32, low / len(cuts), largest / len(cuts))
        loudness = loudness * jnp.repeat(jnp.exp(draws), shape[axis_at] // shards_of).reshape((-1,) + (1,) * (len(shape) - 1 - axis_at))
    return loudness


def scatter_about(own_key, extent, scale, most, cuts=(), kind=jnp.bfloat16):
    drawn = scale * jax.random.normal(own_key, extent, jnp.float32)
    if cuts:
        drawn = drawn * steps_of(own_key, extent, cuts, -0.22, 0.18)
    return jnp.clip(drawn, -most, most).astype(kind)


def bell_draw_with(key, extent, scale, bound, cuts, heavy, kind=jnp.bfloat16):
    entries = scale * jax.random.normal(key, extent, jnp.float32)
    if cuts:
        entries = entries * steps_of(key, extent, cuts, -0.22, 0.18)
    return jnp.clip(spiked(entries, jax.random.fold_in(key, 3), *heavy), -bound, bound).astype(kind)


def setup_inputs(seed: int = 0) -> dict:
    key_list = jax.random.split(jax.random.key(seed), 19)
    residual = scatter_about(key_list[0], (TOKENS, D), 1.0, 6.0, ((0, 32),), jnp.float32)
    segment_ids = draw_segment_ids(jax.random.fold_in(key_list[18], 71), 0)
    live_counts = draw_live_counts(jax.random.fold_in(key_list[18], 71), 0)
    norm_gain = jnp.clip(1.0 + 0.1 * jax.random.normal(key_list[3], (D,), jnp.float32), 0.5, 1.5)
    z_weight = scatter_about(key_list[4], (D, INNER), D ** -0.5, 0.1875, ((0, 16), (1, 2)))
    x_weight = scatter_about(key_list[5], (D, INNER), D ** -0.5, 0.1875, ((0, 16), (1, 2)))
    bc_weight = scatter_about(key_list[6], (D, 2 * STATE), D ** -0.5, 0.1875, ((0, 16),))
    dt_weight = scatter_about(key_list[7], (D, HEADS), D ** -0.5, 0.1875, ((0, 16), (1, 2)))
    conv_x = scatter_about(key_list[8], (CONV, INNER), CONV ** -0.5, 3.0, ((1, 2),), jnp.float32)
    conv_x_bias = scatter_about(key_list[9], (INNER,), 0.5, 3.0, ((0, 2),), jnp.float32)
    conv_bc = scatter_about(key_list[10], (CONV, 2 * STATE), CONV ** -0.5, 3.0, (), jnp.float32)
    conv_bc_bias = scatter_about(key_list[11], (2 * STATE,), 0.5, 3.0, (), jnp.float32)
    dt_bias = jnp.clip(-6.9 + 4.6000001430511475 * jax.random.uniform(key_list[12], (HEADS,), jnp.float32) ** steps_of(key_list[12], (HEADS,), ((0, 2),), -0.2, 0.2), -6.9, -2.3)
    a_log = jnp.clip(2.77 * jax.random.uniform(key_list[13], (HEADS,), jnp.float32) ** steps_of(key_list[13], (HEADS,), ((0, 2),), -0.2, 0.2), 0.0, 2.77)
    d_skip = jnp.clip(0.5 + 1.0 * jax.random.uniform(key_list[14], (HEADS,), jnp.float32) ** steps_of(key_list[14], (HEADS,), ((0, 2),), -0.2, 0.2), 0.5, 1.5)
    gate_gain = jnp.clip(1.0 + 0.1 * jax.random.normal(key_list[15], (INNER,), jnp.float32), 0.5, 1.5)
    out_weight = scatter_about(key_list[16], (INNER, D), INNER ** -0.5, 0.125, ((0, 2), (1, 16)))
    cotangent = bell_draw_with(key_list[17], (TOKENS, D), 1.0, 6.0, ((0, 32),), (0, 1, 32, 2.75), jnp.float32)
    return dict(residual=residual, segment_ids=segment_ids, live_counts=live_counts, norm_gain=norm_gain, z_weight=z_weight, x_weight=x_weight, bc_weight=bc_weight, dt_weight=dt_weight, conv_x=conv_x, conv_x_bias=conv_x_bias, conv_bc=conv_bc, conv_bc_bias=conv_bc_bias, dt_bias=dt_bias, a_log=a_log, d_skip=d_skip, gate_gain=gate_gain, out_weight=out_weight, cotangent=cotangent)


epsilon = 1e-05

def causal_conv(values, kernel, bias_vec, segment):
    width = kernel.shape[0]
    row_total = values.shape[0]
    result = bias_vec + kernel[width - 1] * values
    for lag_steps in range(1, width):
        moved = jnp.concatenate([jnp.zeros((lag_steps, values.shape[1]), values.dtype), values[:row_total - lag_steps]], 0)
        seg_moved = jnp.concatenate([jnp.full((lag_steps,), -1, jnp.int32), segment[:row_total - lag_steps].astype(jnp.int32)])
        linked = (segment.astype(jnp.int32) == seg_moved).astype(values.dtype)
        result = result + kernel[width - 1 - lag_steps] * moved * linked[:, None]
    return result

def ssd_core(segment, block_len, z_pre, x_pre, bc_pre, dt_pre, conv_x, conv_x_bias, conv_bc, conv_bc_bias, dt_bias, a_log, d_skip):
    row_total, head_count = dt_pre.shape
    head_width = x_pre.shape[1] // head_count
    state_size = bc_pre.shape[1] // 2
    highest = lax.Precision.HIGHEST
    x_conv = jax.nn.silu(causal_conv(x_pre, conv_x, conv_x_bias, segment))
    bc_conv = jax.nn.silu(causal_conv(bc_pre, conv_bc, conv_bc_bias, segment))
    b_input = bc_conv[:, :state_size]
    c_output = bc_conv[:, state_size:]
    step_sizes = jax.nn.softplus(dt_pre + dt_bias)
    log_decay = -step_sizes * jnp.exp(a_log)
    x_heads = x_conv.reshape(row_total, head_count, head_width)
    carry_state = jnp.zeros((head_count, head_width, state_size), x_conv.dtype)
    prev_segment = segment[0]
    positions = jnp.arange(block_len)
    lower_tri = positions[:, None] >= positions[None, :]
    pieces = []
    for first_row in range(0, row_total, block_len):
        block_seg = segment[first_row:first_row + block_len]
        block_step = step_sizes[first_row:first_row + block_len]
        block_x = x_heads[first_row:first_row + block_len]
        block_b = b_input[first_row:first_row + block_len]
        block_c = c_output[first_row:first_row + block_len]
        cumulative = jnp.cumsum(log_decay[first_row:first_row + block_len], axis=0)
        within = (block_seg[:, None] == block_seg[None, :]) & lower_tri
        gaps_log = cumulative.T[:, :, None] - cumulative.T[:, None, :]
        within_f = within.astype(x_conv.dtype)[None]
        decay_mat = jnp.exp(jnp.where(within[None], gaps_log, 0.0)) * within_f
        scores = jnp.dot(block_c, block_b.T, precision=highest)
        weighted = decay_mat * scores[None] * block_step.T[:, None, :]
        y_within = jnp.einsum('hts,shp->thp', weighted, block_x, precision=highest)
        keep_prev = (block_seg == prev_segment).astype(x_conv.dtype)
        carried_scale = jnp.exp(cumulative) * keep_prev[:, None]
        y_carried = jnp.einsum('tn,hpn->thp', block_c, carry_state, precision=highest) * carried_scale[:, :, None]
        pieces.append(y_within + y_carried)
        last_log = cumulative[-1]
        tail_mask = (block_seg == block_seg[-1]).astype(x_conv.dtype)
        state_coef = jnp.exp(last_log[None, :] - cumulative) * tail_mask[:, None] * block_step
        carry_state = carry_state * (jnp.exp(last_log) * keep_prev[-1])[:, None, None] + jnp.einsum('sh,shp,sn->hpn', state_coef, block_x, block_b, precision=highest)
        prev_segment = block_seg[-1]
    y_all = jnp.concatenate(pieces, 0) + d_skip[None, :, None] * x_heads
    return y_all.reshape(row_total, head_count * head_width) * jax.nn.silu(z_pre)

def reference(residual, segment_ids, live_counts, norm_gain, z_weight, x_weight, bc_weight, dt_weight, conv_x, conv_x_bias, conv_bc, conv_bc_bias, dt_bias, a_log, d_skip, gate_gain, out_weight, cotangent):
    group_heads = HEADS // N_TENSOR
    group_inner = INNER // N_TENSOR
    f32 = jnp.float32

    def per_stream(totals, inputs):
        resid, cotan, segment, count_live = inputs
        inv_rms = lax.rsqrt(lax.optimization_barrier(jnp.mean(resid * resid, axis=1)) + epsilon)
        normed = (resid * inv_rms[:, None] * norm_gain).astype(jnp.bfloat16)
        z_pre = jnp.dot(normed, z_weight, preferred_element_type=jnp.float32)
        x_pre = jnp.dot(normed, x_weight, preferred_element_type=jnp.float32)
        bc_pre = jnp.dot(normed, bc_weight, preferred_element_type=jnp.float32)
        dt_pre = jnp.dot(normed, dt_weight, preferred_element_type=jnp.float32)
        core = partial(ssd_core, segment, SPAN)
        gated_parts = []
        backs = []
        for group in range(N_TENSOR):
            lo_c = group * group_inner
            lo_h = group * group_heads
            part_out, part_back = jax.vjp(core, z_pre[:, lo_c:lo_c + group_inner], x_pre[:, lo_c:lo_c + group_inner], bc_pre, dt_pre[:, lo_h:lo_h + group_heads], conv_x[:, lo_c:lo_c + group_inner], conv_x_bias[lo_c:lo_c + group_inner], conv_bc, conv_bc_bias, dt_bias[lo_h:lo_h + group_heads], a_log[lo_h:lo_h + group_heads], d_skip[lo_h:lo_h + group_heads])
            gated_parts.append(part_out)
            backs.append(part_back)
        gated = jnp.concatenate(gated_parts, 1)
        gate_inv = lax.rsqrt(lax.optimization_barrier(jnp.sum(gated * gated, axis=1)) / INNER + epsilon)
        live_mask = (jnp.arange(TOK_DEV) < count_live).astype(gated.dtype)
        mixed = (gated * gate_inv[:, None] * gate_gain * live_mask[:, None]).astype(jnp.bfloat16)
        block_out = resid + jnp.dot(mixed, out_weight, preferred_element_type=jnp.float32)
        cot_b = cotan.astype(jnp.bfloat16)
        out_part = jnp.dot(mixed.T, cot_b, preferred_element_type=jnp.float32)
        d_mixed = jnp.dot(cot_b, out_weight.T, preferred_element_type=jnp.float32)
        d_masked = d_mixed * live_mask[:, None]
        gain_part = lax.optimization_barrier(jnp.sum(d_masked * gated * gate_inv[:, None], axis=0))
        d_scaled = d_masked * gate_gain
        inner_dot = lax.optimization_barrier(jnp.sum(d_scaled * gated, axis=1))
        d_gated = gate_inv[:, None] * d_scaled - gated * (gate_inv ** 3 * inner_dot / INNER)[:, None]
        dz_list, dx_list, ddt_list, dbc_list = ([], [], [], [])
        cx_list, cxb_list, dtb_list, alog_list, skip_list = ([], [], [], [], [])
        conv_bc_part = jnp.zeros(conv_bc.shape, f32)
        conv_bcb_part = jnp.zeros(conv_bc_bias.shape, f32)
        for group in range(N_TENSOR):
            lo_c = group * group_inner
            grads = backs[group](d_gated[:, lo_c:lo_c + group_inner])
            dz_list.append(grads[0])
            dx_list.append(grads[1])
            dbc_list.append(grads[2].astype(jnp.bfloat16))
            ddt_list.append(grads[3])
            cx_list.append(grads[4])
            cxb_list.append(grads[5])
            conv_bc_part = conv_bc_part + grads[6]
            conv_bcb_part = conv_bcb_part + grads[7]
            dtb_list.append(grads[8])
            alog_list.append(grads[9])
            skip_list.append(grads[10])
        dz_b = jnp.concatenate(dz_list, 1).astype(jnp.bfloat16)
        dx_b = jnp.concatenate(dx_list, 1).astype(jnp.bfloat16)
        ddt_b = jnp.concatenate(ddt_list, 1).astype(jnp.bfloat16)
        z_part = jnp.dot(normed.T, dz_b, preferred_element_type=jnp.float32)
        x_part = jnp.dot(normed.T, dx_b, preferred_element_type=jnp.float32)
        dt_part = jnp.dot(normed.T, ddt_b, preferred_element_type=jnp.float32)
        d_normed = jnp.dot(dz_b, z_weight.T, preferred_element_type=jnp.float32) + jnp.dot(dx_b, x_weight.T, preferred_element_type=jnp.float32) + jnp.dot(ddt_b, dt_weight.T, preferred_element_type=jnp.float32)
        bc_part = jnp.zeros(bc_weight.shape, f32)
        for group in range(N_TENSOR):
            bc_part = bc_part + jnp.dot(normed.T, dbc_list[group], preferred_element_type=jnp.float32)
            d_normed = d_normed + jnp.dot(dbc_list[group], bc_weight.T, preferred_element_type=jnp.float32)
        norm_part = lax.optimization_barrier(jnp.sum(d_normed * resid * inv_rms[:, None], axis=0))
        d_gain = d_normed * norm_gain
        input_grad = cotan + inv_rms[:, None] * d_gain - resid * (inv_rms ** 3 * lax.optimization_barrier(jnp.sum(d_gain * resid, axis=1)) / D)[:, None]
        updates = (norm_part, z_part, x_part, bc_part, dt_part, jnp.concatenate(cx_list, 1), jnp.concatenate(cxb_list, 0), conv_bc_part, conv_bcb_part, jnp.concatenate(dtb_list, 0), jnp.concatenate(alog_list, 0), jnp.concatenate(skip_list, 0), gain_part, out_part)
        new_totals = tuple((total + update for total, update in zip(totals, updates)))
        return (new_totals, (block_out, input_grad))
    init_totals = (jnp.zeros((D,), f32), jnp.zeros((D, INNER), f32), jnp.zeros((D, INNER), f32), jnp.zeros((D, 2 * STATE), f32), jnp.zeros((D, HEADS), f32), jnp.zeros((CONV, INNER), f32), jnp.zeros((INNER,), f32), jnp.zeros((CONV, 2 * STATE), f32), jnp.zeros((2 * STATE,), f32), jnp.zeros((HEADS,), f32), jnp.zeros((HEADS,), f32), jnp.zeros((HEADS,), f32), jnp.zeros((INNER,), f32), jnp.zeros((INNER, D), f32))
    stream_inputs = (residual.reshape(STREAMS, TOK_DEV, D), cotangent.reshape(STREAMS, TOK_DEV, D), segment_ids.reshape(STREAMS, TOK_DEV), live_counts)
    totals, per_rows = lax.scan(per_stream, init_totals, stream_inputs)
    block_out = per_rows[0].reshape(TOKENS, D)
    input_grad = per_rows[1].reshape(TOKENS, D)
    return (block_out, input_grad, totals[0], totals[1], totals[2], totals[3], totals[4], totals[5], totals[6], totals[7], totals[8], totals[9], totals[10], totals[11], totals[12], totals[13])
```

```python
import jax
import jax.numpy as jnp
from jax import lax
from jax.experimental import pallas as pl
from jax.experimental.pallas import tpu as pltpu
from jax.sharding import PartitionSpec as P


SPAN = 128
LANES = 128
epsilon = 1e-05
f32 = jnp.float32
bf16 = jnp.bfloat16
HI = lax.Precision.HIGHEST


def dot_nn(a, b, p=None):
    return lax.dot_general(a, b, (((1,), (0,)), ((), ())), precision=p, preferred_element_type=f32)


def dot_nt(a, b, p=None):
    return lax.dot_general(a, b, (((1,), (1,)), ((), ())), precision=p, preferred_element_type=f32)


def dot_tn(a, b, p=None):
    return lax.dot_general(a, b, (((0,), (0,)), ((), ())), precision=p, preferred_element_type=f32)


def call(micros, body, outs, *args, scratch=()):
    return pl.pallas_call(
        body,
        out_shape=[jax.ShapeDtypeStruct(s, d) for s, d in outs],
        scratch_shapes=list(scratch),
        cost_estimate=pl.CostEstimate(
            flops=int(micros * 9e8), transcendentals=0, bytes_accessed=int(micros * 3e6)
        ),
    )(*args)


def paired(a, w, at):
    half = w[0].shape[0]
    return dot_nn(a[:, :half], w[0][:, at]) + dot_nn(a[:, half:], w[1][:, at])


def split(v):
    high = v.astype(bf16)
    return jnp.concatenate([high, (v - high.astype(f32)).astype(bf16)], 0)


def iota(shape, axis):
    return lax.broadcasted_iota(jnp.int32, shape, axis)


def silu(v):
    return v * jax.nn.sigmoid(v)


def silu_slope(v):
    s = jax.nn.sigmoid(v)
    return s * (1.0 + v * (1.0 - s))


def conv(v, w, b, link):
    taps = w.shape[0]
    out = b + w[taps - 1 : taps] * v
    for lag in range(1, taps):
        moved = pltpu.roll(v, lag, 0) * link[:, lag : lag + 1]
        out = out + w[taps - 1 - lag : taps - lag] * moved
    return out


def conv_back(dv, v, w, link):
    taps = w.shape[0]
    rows = v.shape[0]
    dpre = w[taps - 1 : taps] * dv
    dw = [jnp.sum(dv * v, axis=0, keepdims=True)]
    for lag in range(1, taps):
        masked = dv * link[:, lag : lag + 1]
        dw.insert(0, jnp.sum(masked * pltpu.roll(v, lag, 0), axis=0, keepdims=True))
        dpre = dpre + w[taps - 1 - lag : taps - lag] * pltpu.roll(masked, rows - lag, 0)
    return dpre, dw, jnp.sum(dv, axis=0, keepdims=True)


def prepare(dtpre, dtb, alog, segc, segr):
    v = dtpre + dtb
    step = jnp.maximum(v, 0.0) + jnp.log1p(jnp.exp(-jnp.abs(v)))
    logd = -step * jnp.exp(alog)
    row = iota((SPAN, SPAN), 0)
    col = iota((SPAN, SPAN), 1)
    lower = row >= col
    tri = lower.astype(f32)
    cum = [dot_nn(tri, logd[k * SPAN : (k + 1) * SPAN], HI) for k in range(2)]
    cum_t = [c.T for c in cum]
    mask = [
        (segc[k * SPAN : (k + 1) * SPAN] == segr[:, k * SPAN : (k + 1) * SPAN]) & lower
        for k in range(2)
    ]
    edge = segc[SPAN - 1 : SPAN]
    keep = (segc[SPAN:] == edge).astype(f32)
    tail = (segc[:SPAN] == edge).astype(f32)
    grow = jnp.exp(cum[1]) * keep
    coef = jnp.exp(cum[0][SPAN - 1 : SPAN] - cum[0]) * tail
    return v, step, logd, cum, cum_t, mask, grow, coef


def spread(v, first, width):
    lane = iota((v.shape[0], LANES), 1)
    out = jnp.broadcast_to(v[:, first : first + 1], (v.shape[0], LANES))
    for k in range(1, LANES // width):
        out = jnp.where(lane >= k * width, v[:, first + k : first + k + 1], out)
    return out


def decay(cum, cum_t, mask, h):
    return jnp.where(mask, jnp.exp(cum[:, h : h + 1] - cum_t[h : h + 1, :]), 0.0)


def fwd_body(width, nrm, w1a, w1b, link, segc, segr, cx, cxb, cbc, cbcb, dtb, alog,
             xpre_o, xc_o, y_o, bcpre_o, bcc_o, dt_o):
    inner = xc_o.shape[1]
    state = bcc_o.shape[1] // 2
    x = nrm[...]
    w1 = (w1a, w1b)
    pre = paired(x, w1, slice(inner, w1a.shape[1]))
    bcpre_o[...] = pre[:, : 2 * state]
    dt_o[...] = pre[:, 2 * state :]
    wide = 2 * LANES
    for c in range(inner // wide):
        xpre_o[:, c * wide : (c + 1) * wide] = paired(x, w1, slice(c * wide, (c + 1) * wide))
    lk = link[...]
    for c in range(2 * state // LANES):
        at = slice(c * LANES, (c + 1) * LANES)
        bcc_o[:, at] = conv(bcpre_o[:, at], cbc[:, at], cbcb[:, at], lk)
    bs = silu(bcc_o[:, :state])
    cs = silu(bcc_o[:, state:])
    _, step, _, cum, cum_t, mask, grow, coef = prepare(
        dt_o[...], dtb[...], alog[...], segc[...], segr[...]
    )
    scores = [
        dot_nt(cs[k * SPAN : (k + 1) * SPAN], bs[k * SPAN : (k + 1) * SPAN], HI) for k in range(2)
    ]
    b0 = bs[:SPAN].astype(bf16)
    c1 = cs[SPAN:].astype(bf16)
    c1 = jnp.concatenate([c1, c1], 1)
    per = LANES // width
    lane = iota((SPAN, LANES), 1)
    for j in range(inner // LANES):
        at = slice(j * LANES, (j + 1) * LANES)
        xc = conv(xpre_o[:, at], cx[:, at], cxb[:, at], lk)
        xc_o[:, at] = xc
        u = spread(step, j * per, width) * silu(xc)
        ub = u.astype(bf16)
        for k in range(2):
            rows = slice(k * SPAN, (k + 1) * SPAN)
            y = None
            for i in range(per):
                h = j * per + i
                w = (decay(cum[k], cum_t[k], mask[k], h) * scores[k]).astype(bf16)
                part = dot_nn(w, ub[rows])
                y = part if y is None else jnp.where(lane >= i * width, part, y)
            if k:
                kept = (spread(coef, j * per, width) * u[:SPAN]).astype(bf16)
                st = split(dot_tn(b0, kept))
                y = y + spread(grow, j * per, width) * dot_nn(c1, st)
            y_o[rows, at] = y


def as_rows(col):
    return jnp.broadcast_to(col, (col.shape[0], LANES)).T[:8]


def as_col(rows):
    return jnp.broadcast_to(rows[:1], (LANES, rows.shape[1])).T[:, :1]


def dmix_body(cot, outa, outb, live, dm_o):
    wide = 2 * LANES
    x = cot[...]
    lv = live[...]
    for c in range(dm_o.shape[1] // wide):
        at = slice(c * wide, (c + 1) * wide)
        dm_o[:, at] = paired(x, (outa, outb), at) * lv


def gate_body(nrm, wza, wzb, y_r, xc_r, dsk, dm_r, gain, z_o, g_o, sums_o):
    wide = 2 * LANES
    x = nrm[...]
    squares = jnp.zeros((x.shape[0], LANES), f32)
    dots = jnp.zeros((x.shape[0], LANES), f32)
    for c in range(z_o.shape[1] // wide):
        at = slice(c * wide, (c + 1) * wide)
        z_o[:, at] = paired(x, (wza, wzb), at)
    for c in range(z_o.shape[1] // LANES):
        at = slice(c * LANES, (c + 1) * LANES)
        g = (y_r[:, at] + dsk[:, at] * silu(xc_r[:, at])) * silu(z_o[:, at])
        g_o[:, at] = g
        squares = squares + g * g
        dots = dots + dm_r[:, at] * gain[:, at] * g
    sums_o[:8] = as_rows(jnp.sum(squares, axis=1, keepdims=True))
    sums_o[8:] = as_rows(jnp.sum(dots, axis=1, keepdims=True))


def mix_body(full, g_r, sums, sums2, gain, live, cot, outa, outb,
             blk_o, keep_o, send_o, mixed):
    inv = lax.rsqrt(as_col(sums[:8] + sums2[:8]) / full + epsilon)
    wide = 2 * LANES
    for c in range(g_r.shape[1] // LANES):
        at = slice(c * LANES, (c + 1) * LANES)
        mixed[:, at] = (g_r[:, at] * inv * gain[:, at] * live[...]).astype(bf16)
    x = cot[...]
    half = keep_o.shape[0]
    for c in range(g_r.shape[1] // wide):
        at = slice(c * wide, (c + 1) * wide)
        send_o[:, at] = dot_tn(x[:, half:], mixed[:, at]).astype(bf16)
        keep_o[:, at] = dot_tn(x[:, :half], mixed[:, at]).astype(bf16)
    m = mixed[...]
    blk_o[:, :half] = dot_nt(m, outa[...])
    blk_o[:, half:] = dot_nt(m, outb[...])


def dz_body(full, nrm, g_r, dm_r, z_r, y_r, xc_r, dsk, gain, sums, sums2,
            dz_o, dy_o, gp_o, keep_o, send_o):
    inv = lax.rsqrt(as_col(sums[:8] + sums2[:8]) / full + epsilon)
    back = inv * inv * inv * as_col(sums[8:] + sums2[8:]) / full
    for c in range(z_r.shape[1] // LANES):
        at = slice(c * LANES, (c + 1) * LANES)
        z = z_r[:, at]
        s = jax.nn.sigmoid(z)
        g = g_r[:, at]
        dm = dm_r[:, at]
        gp_o[:, at] = jnp.sum(dm * g * inv, axis=0, keepdims=True)
        dg = inv * (dm * gain[:, at]) - g * back
        y = y_r[:, at] + dsk[:, at] * silu(xc_r[:, at])
        dz_o[:, at] = (dg * y * (s * (1.0 + z * (1.0 - s)))).astype(bf16)
        dy_o[:, at] = dg * (z * s)
    x = nrm[...]
    half = keep_o.shape[0]
    wide = 2 * LANES
    for c in range(z_r.shape[1] // wide):
        at = slice(c * wide, (c + 1) * wide)
        send_o[:, at] = dot_tn(x[:, half:], dz_o[:, at]).astype(bf16)
        keep_o[:, at] = dot_tn(x[:, :half], dz_o[:, at]).astype(bf16)


def bwd_body(width, nrm, dy_r, xpre_r, xc_r, y_r, bcpre_r, bcc_r, dt_r, link, segc, segr, cx,
             cbc, dtb, alog, dsk, dx_o, sm_o, keep_o, send_o, dc_s):
    inner = xc_r.shape[1]
    state = bcc_r.shape[1] // 2
    lk = link[...]
    bs = silu(bcc_r[:, :state])
    cs = silu(bcc_r[:, state:])
    v, step, logd, cum, cum_t, mask, grow, coef = prepare(
        dt_r[...], dtb[...], alog[...], segc[...], segr[...]
    )
    scores = [
        dot_nt(cs[k * SPAN : (k + 1) * SPAN], bs[k * SPAN : (k + 1) * SPAN], HI) for k in range(2)
    ]
    b0 = bs[:SPAN].astype(bf16)
    c1 = cs[SPAN:].astype(bf16)
    b00 = jnp.concatenate([b0, b0], 1)
    c11 = jnp.concatenate([c1, c1], 1)
    per = LANES // width
    lane = iota((SPAN, LANES), 1)
    rows_t = 2 * SPAN
    dcum = jnp.zeros((rows_t, LANES), f32)
    dstep = jnp.zeros((rows_t, LANES), f32)
    dsc = [jnp.zeros((SPAN, SPAN), f32) for _ in range(2)]
    dc1 = jnp.zeros((SPAN, state), f32)
    db0 = jnp.zeros((SPAN, state), f32)
    fold_row = iota((LANES, LANES), 0)
    fold_col = iota((LANES, LANES), 1)
    sm_o[...] = jnp.zeros(sm_o.shape, f32)
    for j in range(inner // LANES):
        at = slice(j * LANES, (j + 1) * LANES)
        xc = xc_r[:, at]
        xs = silu(xc)
        se = spread(step, j * per, width)
        u = se * xs
        ub = u.astype(bf16)
        dy = dy_r[:, at]
        dyb = dy.astype(bf16)
        ce = spread(coef, j * per, width)
        ge = spread(grow, j * per, width)
        kept = (ce * u[:SPAN]).astype(bf16)
        st = split(dot_tn(b0, kept))
        zb = (ge * dy[SPAN:]).astype(bf16)
        dst = split(dot_tn(c1, zb))
        dc1 = dc1 + dot_nt(zb, st[:state])
        db0 = db0 + dot_nt(kept, dst[:state])
        over = dot_nn(c11, st)
        under = dot_nn(b00, dst)
        dus = []
        for k in range(2):
            rows = slice(k * SPAN, (k + 1) * SPAN)
            du = None
            for i in range(per):
                h = j * per + i
                dec = decay(cum[k], cum_t[k], mask[k], h)
                w = (dec * scores[k]).astype(bf16)
                part = dot_tn(w, dyb[rows])
                du = part if du is None else jnp.where(lane >= i * width, part, du)
                inside = (lane >= i * width) & (lane < (i + 1) * width)
                mine = jnp.where(inside, dy[rows], 0.0).astype(bf16)
                dsc[k] = dsc[k] + dec * dot_nt(mine, ub[rows])
            dus.append(du)
        ubf = ub.astype(f32)
        dyf = dyb.astype(f32)
        net = jnp.concatenate(
            [
                dyf[:SPAN] * y_r[:SPAN, at] - ubf[:SPAN] * dus[0] - kept.astype(f32) * under,
                dyf[SPAN:] * (y_r[SPAN:, at] - ge * over) + zb.astype(f32) * over
                - ubf[SPAN:] * dus[1],
            ],
            0,
        )
        du = jnp.concatenate([dus[0] + ce * under, dus[1]], 0)
        fold = (fold_col == j * per + fold_row // width).astype(f32)
        dcum = dcum + dot_nn(net, fold, HI)
        dstep = dstep + dot_nn(du * xs, fold, HI)
        sm_o[6:7, at] = jnp.sum(dy * xs, axis=0, keepdims=True)
        dxc = (du * se + dsk[:, at] * dy) * silu_slope(xc)
        dpre, dw, db = conv_back(dxc, xpre_r[:, at], cx[:, at], lk)
        dx_o[:, at] = dpre.astype(bf16)
        for k, piece in enumerate(dw):
            sm_o[k : k + 1, at] = piece
        sm_o[4:5, at] = db
    upper = (iota((rows_t, rows_t), 0) <= iota((rows_t, rows_t), 1)) & (segc[...] == segr[...])
    dlog = dot_nn(upper.astype(f32), dcum, HI)
    ddt = (dstep - dlog * jnp.exp(alog[...])) * jax.nn.sigmoid(v)
    dx_o[:, inner + 2 * state :] = ddt.astype(bf16)
    sm_o[7:8, :LANES] = jnp.sum(ddt, axis=0, keepdims=True)
    sm_o[7:8, LANES : 2 * LANES] = jnp.sum(dlog * logd, axis=0, keepdims=True)
    for k in range(2):
        rows = slice(k * SPAN, (k + 1) * SPAN)
        db = dot_tn(dsc[k], cs[rows], HI)
        dc = dot_nn(dsc[k], bs[rows], HI)
        if k == 0:
            db = db + db0
        else:
            dc = dc + dc1
        dc_s[rows, :state] = db
        dc_s[rows, state:] = dc
    for c in range(2 * state // LANES):
        at = slice(c * LANES, (c + 1) * LANES)
        dpre, dw, db = conv_back(
            dc_s[:, at] * silu_slope(bcc_r[:, at]), bcpre_r[:, at], cbc[:, at], lk
        )
        dx_o[:, inner + c * LANES : inner + (c + 1) * LANES] = dpre.astype(bf16)
        for k, piece in enumerate(dw):
            sm_o[8 + k : 9 + k, at] = piece
        sm_o[12:13, at] = db
    x = nrm[...]
    wide = keep_o.shape[1]
    half = keep_o.shape[0]
    for first in range(0, wide, 2 * LANES):
        at = slice(first, min(first + 2 * LANES, wide))
        send_o[:, at] = dot_tn(x[:, half:], dx_o[:, at]).astype(bf16)
        keep_o[:, at] = dot_tn(x[:, :half], dx_o[:, at]).astype(bf16)


def dn_body(dz, wza, wzb, dx, w1a, w1b, dn_o):
    a = dz[...]
    b = dx[...]
    half = wza.shape[0]
    dn_o[:, :half] = dot_nt(a, wza[...]) + dot_nt(b, w1a[...])
    dn_o[:, half:] = dot_nt(a, wzb[...]) + dot_nt(b, w1b[...])


def restore(v, place):
    high = v.astype(bf16)
    low = (v - high.astype(f32)).astype(bf16)
    return dot_nt(high, place) + dot_nt(low, place)


def block_body(res, own, other, place, out_o):
    out_o[...] = res[...] + restore(own[...] + other[...].astype(f32), place[...])


def tail_body(res, cot, gain, own, other, place, ig_o, np_o):
    r = res[...]
    dn = restore(own[...] + other[...].astype(f32), place[...])
    inv = lax.rsqrt(jnp.mean(r * r, axis=1, keepdims=True) + epsilon)
    np_o[...] = jnp.sum(dn * r * inv, axis=0, keepdims=True)
    dg = dn * gain[...]
    inner = jnp.sum(dg * r, axis=1, keepdims=True) / r.shape[1]
    ig_o[...] = cot[...] + inv * dg - r * (inv * inv * inv * inner)


def head_body(res, cot, gain, place, nrm_o, cot_o):
    r = res[...]
    inv = lax.rsqrt(jnp.mean(r * r, axis=1, keepdims=True) + epsilon)
    n = (r * inv * gain[...]).astype(bf16)
    nrm_o[...] = dot_nn(n, place[...]).astype(bf16)
    cot_o[...] = dot_nn(cot[...].astype(bf16), place[...]).astype(bf16)


def solution(mesh):
    n = mesh.shape["dp"]
    nt = mesh.shape["tensor"]
    bits = [1 << k for k in range(n.bit_length() - 1)]
    assert (1 << len(bits)) == n and nt == 2

    def swap(v, bit):
        return lax.ppermute(v, "dp", [(i, i ^ bit) for i in range(n)])

    def cross(v):
        return lax.ppermute(v, "tensor", [(0, 1), (1, 0)])

    def after(v, *others):
        return lax.optimization_barrier((v,) + others)[0]

    def gather(v, start):
        if start is not None:
            v = after(v, start)
        marks = []
        for bit in reversed(bits):
            r = swap(v, bit)
            marks.append(r)
            if bit > 1:
                v = jnp.concatenate([v, r], 0)
        return v, r, marks

    def plus(a, b):
        return a.astype(f32) + b.astype(f32)

    def scatter(keep, send):
        for bit in bits[:-1]:
            r = swap(send, bit)
            half = keep.shape[0] // 2
            send = plus(keep[half:], r[half:]).astype(bf16)
            keep = plus(keep[:half], r[:half]).astype(bf16)
        return plus(keep, swap(send, bits[-1]))

    def whole(residual, segment_ids, live_counts, norm_gain, z_weight, x_weight, bc_weight,
              dt_weight, conv_x, conv_x_bias, conv_bc, conv_bc_bias, dt_bias, a_log, d_skip,
              gate_gain, out_weight, cotangent):
        half, width_d = residual.shape
        tokens = segment_ids.shape[0]
        inner = x_weight.shape[1]
        heads = dt_weight.shape[1]
        two_state = bc_weight.shape[1]
        head_width = inner // heads
        full = float(inner * nt)
        shard = width_d // n
        me = lax.axis_index("dp")
        side = lax.axis_index("tensor")

        pad = LANES - heads
        w1s = jnp.concatenate([x_weight, bc_weight, jnp.pad(dt_weight, ((0, 0), (0, pad)))], 1)
        outa, outb, m1 = gather(out_weight.T, None)
        w1a, w1b, m2 = gather(w1s, m1[1])
        wza, wzb, _ = gather(z_weight, m2[1])

        spot = jnp.arange(width_d, dtype=jnp.int32)
        block = spot // shard
        turned = jnp.zeros_like(block)
        for k in range(len(bits)):
            turned = turned | (((block >> k) & 1) << (len(bits) - 1 - k))
        source = (turned ^ me) * shard + spot % shard
        place = (spot[:, None] == source[None, :]).astype(bf16)

        gain = norm_gain[None, :]
        nrm_half, cot_half = call(
            3.5, head_body, [((half, width_d), bf16)] * 2, residual, cotangent, gain, place
        )

        def both(own, other):
            first = jnp.where(side == 0, own, other)
            second = jnp.where(side == 0, other, own)
            return jnp.concatenate([first, second], 0)

        nrm_other = cross(nrm_half)
        nrm = both(nrm_half, nrm_other)
        cot = both(cot_half, cross(after(cot_half, nrm_other)))

        spots = jnp.arange(tokens)
        links = [jnp.ones((tokens,), f32)]
        for lag in range(1, conv_x.shape[0]):
            moved = jnp.concatenate(
                [jnp.full((lag,), -1, jnp.int32), segment_ids[: tokens - lag]]
            )
            links.append((segment_ids == moved).astype(f32))
        link = jnp.stack(links, 1)
        segc = segment_ids[:, None]
        segr = segment_ids[None, :]
        live = (spots < live_counts[0]).astype(f32)[:, None]
        dtb = jnp.pad(dt_bias, (0, pad))[None, :]
        alog = jnp.pad(a_log, (0, pad))[None, :]
        dsk = jnp.repeat(d_skip, head_width)[None, :]
        gg = gate_gain[None, :]
        cxb = conv_x_bias[None, :]
        cbcb = conv_bc_bias[None, :]

        big = ((tokens, inner), f32)

        def fwd(*a):
            return fwd_body(head_width, *a)

        (dm,) = call(3.0, dmix_body, [big], cot, outa, outb, live)
        xpre, xc, y, bcpre, bcc, dtp = call(
            7.0, fwd,
            [big, big, big, ((tokens, two_state), f32), ((tokens, two_state), f32),
             ((tokens, LANES), f32)],
            nrm, w1a, w1b, link, segc, segr, conv_x, cxb, conv_bc, cbcb, dtb, alog,
        )
        z, g, sums = call(
            5.0, gate_body, [big, big, ((16, tokens), f32)],
            nrm, wza, wzb, y, xc, dsk, dm, gg,
        )
        sums2 = cross(sums)

        def mix(*a):
            return mix_body(full, *a)

        cut = width_d // 2
        blk, out_keep, out_send = call(
            4.0, mix,
            [((tokens, width_d), f32), ((cut, inner), bf16), ((cut, inner), bf16)],
            g, sums, sums2, gg, live, cot, outa, outb,
            scratch=[pltpu.VMEM((tokens, inner), bf16)],
        )
        out_sum = scatter(out_keep, out_send)

        def mine(v):
            return lax.dynamic_slice_in_dim(v, side * half, half, 0)

        def theirs(v):
            return lax.dynamic_slice_in_dim(v, (1 - side) * half, half, 0).astype(bf16)

        blk_other = cross(theirs(blk))
        (block_out,) = call(
            2.5, block_body, [((half, width_d), f32)], residual, mine(blk), blk_other, place
        )

        def back_z(*a):
            return dz_body(full, *a)

        dz, dy, gain_part, z_keep, z_send = call(
            6.0, back_z,
            [((tokens, inner), bf16), big, ((1, inner), f32), ((cut, inner), bf16),
             ((cut, inner), bf16)],
            after(nrm, out_send), g, dm, z, y, xc, dsk, gg, sums, sums2,
        )
        z_weight_grad = scatter(z_keep, z_send)

        def back(*a):
            return bwd_body(head_width, *a)

        wide = w1a.shape[1]
        dx, small, x_keep, x_send = call(
            14.0, back,
            [((tokens, wide), bf16), ((16, inner), f32), ((cut, wide), bf16), ((cut, wide), bf16)],
            nrm, dy, xpre, xc, y, bcpre, bcc, dtp, link, segc, segr, conv_x, conv_bc, dtb, alog,
            dsk,
            scratch=[pltpu.VMEM((tokens, two_state), f32)],
        )
        sum1 = scatter(x_keep, x_send)
        x_weight_grad = sum1[:, :inner]
        dt_weight_grad = sum1[:, inner + two_state : inner + two_state + heads]
        bc = sum1[:, inner : inner + two_state].reshape(nt, shard // nt, two_state)
        bc_weight_grad = (
            lax.dynamic_index_in_dim(bc, side, 0, False)
            + cross(lax.dynamic_index_in_dim(bc, 1 - side, 0, False))
        )

        (dn,) = call(5.5, dn_body, [((tokens, width_d), f32)], dz, wza, wzb, dx, w1a, w1b)
        dn_other = cross(theirs(dn))
        input_grad, norm_part = call(
            4.0, tail_body, [((half, width_d), f32), ((1, width_d), f32)],
            residual, cotangent, gain, mine(dn), dn_other, place,
        )

        few = jnp.concatenate(
            [small[:5], gain_part, small[6:13], norm_part], 0
        )
        few = jnp.concatenate([few[:8], few[13:14], few[8:13], few[:2]], 0)
        for bit in bits:
            few = few + swap(few, bit)
        shared = few[8:16]
        shared = shared + cross(shared)
        return (
            block_out,
            input_grad,
            shared[0],
            z_weight_grad,
            x_weight_grad,
            bc_weight_grad,
            dt_weight_grad,
            few[:4],
            few[4],
            shared[1:5, :two_state],
            shared[5, :two_state],
            few[7, :heads],
            few[7, LANES : LANES + heads],
            jnp.sum(few[6].reshape(heads, head_width), axis=1),
            few[5],
            out_sum.T,
        )

    placed = (
        P(("dp", "tensor"), None),
        P("dp"),
        P("dp"),
        P(),
        P("dp", "tensor"),
        P("dp", "tensor"),
        P("dp", None),
        P("dp", "tensor"),
        P(None, "tensor"),
        P("tensor"),
        P(),
        P(),
        P("tensor"),
        P("tensor"),
        P("tensor"),
        P("tensor"),
        P("tensor", "dp"),
        P(("dp", "tensor"), None),
    )

    return jax.shard_map(
        whole,
        mesh=mesh,
        in_specs=placed,
        out_specs=(
            P(("dp", "tensor"), None),
            P(("dp", "tensor"), None),
            P(),
            P("dp", "tensor"),
            P("dp", "tensor"),
            P(("dp", "tensor"), None),
            P("dp", "tensor"),
            P(None, "tensor"),
            P("tensor"),
            P(),
            P(),
            P("tensor"),
            P("tensor"),
            P("tensor"),
            P("tensor"),
            P("tensor", "dp"),
        ),
        check_vma=False,
    )
```

```python
import jax
import jax.numpy as jnp
from jax import lax
from jax.experimental import pallas as pl
from jax.experimental.pallas import tpu as pltpu
from jax.sharding import PartitionSpec as P


SPAN = 128
LANES = 128
VMEM = 20 * 1024 * 1024
epsilon = 1e-05
f32 = jnp.float32
bf16 = jnp.bfloat16
HI = lax.Precision.HIGHEST


def dot_nn(a, b, p=None):
    return lax.dot_general(a, b, (((1,), (0,)), ((), ())), precision=p, preferred_element_type=f32)


def dot_nt(a, b, p=None):
    return lax.dot_general(a, b, (((1,), (1,)), ((), ())), precision=p, preferred_element_type=f32)


def dot_tn(a, b, p=None):
    return lax.dot_general(a, b, (((0,), (0,)), ((), ())), precision=p, preferred_element_type=f32)


def call(micros, body, outs, *args, scratch=(), scalars=0):
    return pl.pallas_call(
        body,
        out_shape=[jax.ShapeDtypeStruct(s, d) for s, d in outs],
        in_specs=[pl.BlockSpec(memory_space=pltpu.SMEM)] * scalars
        + [pl.BlockSpec(memory_space=pltpu.VMEM)] * (len(args) - scalars),
        scratch_shapes=list(scratch),
        cost_estimate=pl.CostEstimate(
            flops=int(micros * 9e8), transcendentals=0, bytes_accessed=int(micros * 3e6)
        ),
        compiler_params=pltpu.CompilerParams(vmem_limit_bytes=VMEM),
    )(*args)


def paired(a, w, at):
    half = w[0].shape[0]
    return dot_nn(a[:, :half], w[0][:, at]) + dot_nn(a[:, half:], w[1][:, at])


def split(v):
    high = v.astype(bf16)
    return jnp.concatenate([high, (v - high.astype(f32)).astype(bf16)], 0)


def halves(v):
    high = v.astype(bf16)
    return jnp.concatenate([high, (v - high.astype(f32)).astype(bf16)], 1)


def rows_of(side, half):
    return pl.ds(pl.multiple_of(side * half, half), half)


def iota(shape, axis):
    return lax.broadcasted_iota(jnp.int32, shape, axis)


def silu(v):
    return v * jax.nn.sigmoid(v)


def silu_slope(v):
    s = jax.nn.sigmoid(v)
    return s * (1.0 + v * (1.0 - s))


def conv(v, w, b, link):
    taps = w.shape[0]
    out = b + w[taps - 1 : taps] * v
    for lag in range(1, taps):
        moved = pltpu.roll(v, lag, 0) * link[:, lag : lag + 1]
        out = out + w[taps - 1 - lag : taps - lag] * moved
    return out


def conv_back(dv, v, w, link):
    taps = w.shape[0]
    rows = v.shape[0]
    dpre = w[taps - 1 : taps] * dv
    dw = [jnp.sum(dv * v, axis=0, keepdims=True)]
    for lag in range(1, taps):
        masked = dv * link[:, lag : lag + 1]
        dw.insert(0, jnp.sum(masked * pltpu.roll(v, lag, 0), axis=0, keepdims=True))
        dpre = dpre + w[taps - 1 - lag : taps - lag] * pltpu.roll(masked, rows - lag, 0)
    return dpre, dw, jnp.sum(dv, axis=0, keepdims=True)


def prepare(dtpre, dtb, alog, segc, segr):
    v = dtpre + dtb
    step = jnp.maximum(v, 0.0) + jnp.log1p(jnp.exp(-jnp.abs(v)))
    logd = -step * jnp.exp(alog)
    row = iota((SPAN, SPAN), 0)
    col = iota((SPAN, SPAN), 1)
    lower = row >= col
    tri = lower.astype(f32)
    cum = [dot_nn(tri, logd[k * SPAN : (k + 1) * SPAN], HI) for k in range(2)]
    cum_t = [c.T for c in cum]
    mask = [
        (segc[k * SPAN : (k + 1) * SPAN] == segr[:, k * SPAN : (k + 1) * SPAN]) & lower
        for k in range(2)
    ]
    edge = segc[SPAN - 1 : SPAN]
    keep = (segc[SPAN:] == edge).astype(f32)
    tail = (segc[:SPAN] == edge).astype(f32)
    grow = jnp.exp(cum[1]) * keep
    coef = jnp.exp(cum[0][SPAN - 1 : SPAN] - cum[0]) * tail
    return v, step, logd, cum, cum_t, mask, grow, coef


def spread(v, first, width):
    lane = iota((v.shape[0], LANES), 1)
    out = jnp.broadcast_to(v[:, first : first + 1], (v.shape[0], LANES))
    for k in range(1, LANES // width):
        out = jnp.where(lane >= k * width, v[:, first + k : first + k + 1], out)
    return out


def decay(cum, cum_t, mask, h):
    return jnp.where(mask, jnp.exp(cum[:, h : h + 1] - cum_t[h : h + 1, :]), 0.0)


def fwd_body(width, nrm, w1a, w1b, link, segc, segr, cx, cxb, cbc, cbcb, dtb, alog,
             xpre_o, xc_o, y_o, bcpre_o, bcc_o, dt_o, dec_o):
    inner = xc_o.shape[1]
    state = bcc_o.shape[1] // 2
    x = nrm[...]
    w1 = (w1a, w1b)
    pre = paired(x, w1, slice(inner, w1a.shape[1]))
    bcpre_o[...] = pre[:, : 2 * state]
    dt_o[...] = pre[:, 2 * state :]
    wide = 2 * LANES
    for c in range(inner // wide):
        xpre_o[:, c * wide : (c + 1) * wide] = paired(x, w1, slice(c * wide, (c + 1) * wide))
    lk = link[...]
    for c in range(2 * state // LANES):
        at = slice(c * LANES, (c + 1) * LANES)
        bcc_o[:, at] = conv(bcpre_o[:, at], cbc[:, at], cbcb[:, at], lk)
    bs = silu(bcc_o[:, :state])
    cs = silu(bcc_o[:, state:])
    _, step, _, cum, cum_t, mask, grow, coef = prepare(
        dt_o[...], dtb[...], alog[...], segc[...], segr[...]
    )
    scores = [
        dot_nt(cs[k * SPAN : (k + 1) * SPAN], bs[k * SPAN : (k + 1) * SPAN], HI) for k in range(2)
    ]
    b0 = bs[:SPAN].astype(bf16)
    c1 = cs[SPAN:].astype(bf16)
    c1 = jnp.concatenate([c1, c1], 1)
    per = LANES // width
    lane = iota((SPAN, LANES), 1)
    for j in range(inner // LANES):
        at = slice(j * LANES, (j + 1) * LANES)
        xc = conv(xpre_o[:, at], cx[:, at], cxb[:, at], lk)
        xc_o[:, at] = xc
        u = spread(step, j * per, width) * silu(xc)
        ub = u.astype(bf16)
        for k in range(2):
            rows = slice(k * SPAN, (k + 1) * SPAN)
            y = None
            for i in range(per):
                h = j * per + i
                dec = decay(cum[k], cum_t[k], mask[k], h)
                dec_o[2 * h + k] = dec
                w = (dec * scores[k]).astype(bf16)
                part = dot_nn(w, ub[rows])
                y = part if y is None else jnp.where(lane >= i * width, part, y)
            if k:
                kept = (spread(coef, j * per, width) * u[:SPAN]).astype(bf16)
                st = split(dot_tn(b0, kept))
                y = y + spread(grow, j * per, width) * dot_nn(c1, st)
            y_o[rows, at] = y


def as_rows(col):
    return jnp.broadcast_to(col, (col.shape[0], LANES)).T[:8]


def as_col(rows):
    return jnp.broadcast_to(rows[:1], (LANES, rows.shape[1])).T[:, :1]


def dmix_body(cot, outa, outb, live, dm_o):
    wide = 2 * LANES
    x = cot[...]
    lv = live[...]
    for c in range(dm_o.shape[1] // wide):
        at = slice(c * wide, (c + 1) * wide)
        dm_o[:, at] = paired(x, (outa, outb), at) * lv


def gate_body(nrm, wza, wzb, y_r, xc_r, dsk, dm_r, gain, z_o, g_o, sums_o):
    wide = 2 * LANES
    x = nrm[...]
    squares = jnp.zeros((x.shape[0], LANES), f32)
    dots = jnp.zeros((x.shape[0], LANES), f32)
    for c in range(z_o.shape[1] // wide):
        at = slice(c * wide, (c + 1) * wide)
        z_o[:, at] = paired(x, (wza, wzb), at)
    for c in range(z_o.shape[1] // LANES):
        at = slice(c * LANES, (c + 1) * LANES)
        g = (y_r[:, at] + dsk[:, at] * silu(xc_r[:, at])) * silu(z_o[:, at])
        g_o[:, at] = g
        squares = squares + g * g
        dots = dots + dm_r[:, at] * gain[:, at] * g
    sums_o[:8] = as_rows(jnp.sum(squares, axis=1, keepdims=True))
    sums_o[8:] = as_rows(jnp.sum(dots, axis=1, keepdims=True))


def mix_body(full, g_r, sums, sums2, gain, live, cot_t, keep_o, send_o, mixed):
    inv = lax.rsqrt(as_col(sums[:8] + sums2[:8]) / full + epsilon)
    wide = 2 * LANES
    for c in range(g_r.shape[1] // LANES):
        at = slice(c * LANES, (c + 1) * LANES)
        mixed[:, at] = (g_r[:, at] * inv * gain[:, at] * live[...]).astype(bf16)
    half = keep_o.shape[0]
    for c in range(g_r.shape[1] // wide):
        at = slice(c * wide, (c + 1) * wide)
        send_o[:, at] = dot_nn(cot_t[half:], mixed[:, at]).astype(bf16)
        keep_o[:, at] = dot_nn(cot_t[:half], mixed[:, at]).astype(bf16)


def blk_body(side, mixed, outa, outb, own_o, other_o):
    half = outa.shape[0]
    count = own_o.shape[0]
    m = mixed[rows_of(1 - side[0], count), :]
    other_o[:, :half] = dot_nt(m, outa[...]).astype(bf16)
    other_o[:, half:] = dot_nt(m, outb[...]).astype(bf16)
    m = mixed[rows_of(side[0], count), :]
    own_o[:, :half] = dot_nt(m, outa[...])
    own_o[:, half:] = dot_nt(m, outb[...])


def dz_body(full, nrm_t, g_r, dm_r, z_r, y_r, xc_r, dsk, gain, sums, sums2,
            dz_o, dy_o, gp_o, keep_o, send_o):
    inv = lax.rsqrt(as_col(sums[:8] + sums2[:8]) / full + epsilon)
    back = inv * inv * inv * as_col(sums[8:] + sums2[8:]) / full
    for c in range(z_r.shape[1] // LANES):
        at = slice(c * LANES, (c + 1) * LANES)
        z = z_r[:, at]
        s = jax.nn.sigmoid(z)
        g = g_r[:, at]
        dm = dm_r[:, at]
        gp_o[:, at] = jnp.sum(dm * g * inv, axis=0, keepdims=True)
        dg = inv * (dm * gain[:, at]) - g * back
        y = y_r[:, at] + dsk[:, at] * silu(xc_r[:, at])
        dz_o[:, at] = (dg * y * (s * (1.0 + z * (1.0 - s)))).astype(bf16)
        dy_o[:, at] = dg * (z * s)
    half = keep_o.shape[0]
    wide = 2 * LANES
    for c in range(z_r.shape[1] // wide):
        at = slice(c * wide, (c + 1) * wide)
        send_o[:, at] = dot_nn(nrm_t[half:], dz_o[:, at]).astype(bf16)
        keep_o[:, at] = dot_nn(nrm_t[:half], dz_o[:, at]).astype(bf16)


def bwd_body(width, nrm_t, dy_r, xpre_r, xc_r, y_r, bcpre_r, bcc_r, dt_r, dec_r, link, segc, segr, cx,
             cbc, dtb, alog, dsk, dx_o, sm_o, keep_o, send_o, dc_s):
    inner = xc_r.shape[1]
    state = bcc_r.shape[1] // 2
    lk = link[...]
    bs = silu(bcc_r[:, :state])
    cs = silu(bcc_r[:, state:])
    v, step, logd, _, _, _, grow, coef = prepare(
        dt_r[...], dtb[...], alog[...], segc[...], segr[...]
    )
    scores = [
        dot_nt(cs[k * SPAN : (k + 1) * SPAN], bs[k * SPAN : (k + 1) * SPAN], HI) for k in range(2)
    ]
    b0 = bs[:SPAN].astype(bf16)
    c1 = cs[SPAN:].astype(bf16)
    b00 = jnp.concatenate([b0, b0], 1)
    c11 = jnp.concatenate([c1, c1], 1)
    per = LANES // width
    lane = iota((SPAN, LANES), 1)
    rows_t = 2 * SPAN
    dcum = jnp.zeros((rows_t, LANES), f32)
    dstep = jnp.zeros((rows_t, LANES), f32)
    dskip = jnp.zeros((8, LANES), f32)
    dsc = [jnp.zeros((SPAN, SPAN), f32) for _ in range(2)]
    dc1 = jnp.zeros((SPAN, state), f32)
    db0 = jnp.zeros((SPAN, state), f32)
    fold_row = iota((2 * LANES, LANES), 0) % LANES
    fold_col = iota((2 * LANES, LANES), 1)
    sm_o[...] = jnp.zeros(sm_o.shape, f32)
    for j in range(inner // LANES):
        at = slice(j * LANES, (j + 1) * LANES)
        xc = xc_r[:, at]
        xs = silu(xc)
        se = spread(step, j * per, width)
        u = se * xs
        ub = u.astype(bf16)
        dy = dy_r[:, at]
        dyb = dy.astype(bf16)
        ce = spread(coef, j * per, width)
        ge = spread(grow, j * per, width)
        kept = (ce * u[:SPAN]).astype(bf16)
        st = split(dot_tn(b0, kept))
        zb = (ge * dy[SPAN:]).astype(bf16)
        dst = split(dot_tn(c1, zb))
        dc1 = dc1 + dot_nt(zb, st[:state])
        db0 = db0 + dot_nt(kept, dst[:state])
        over = dot_nn(c11, st)
        under = dot_nn(b00, dst)
        dus = []
        for k in range(2):
            rows = slice(k * SPAN, (k + 1) * SPAN)
            du = None
            for i in range(per):
                h = j * per + i
                dec = dec_r[2 * h + k]
                w = (dec * scores[k]).astype(bf16)
                part = dot_tn(w, dyb[rows])
                du = part if du is None else jnp.where(lane >= i * width, part, du)
                inside = (lane >= i * width) & (lane < (i + 1) * width)
                mine = jnp.where(inside, dy[rows], 0.0).astype(bf16)
                dsc[k] = dsc[k] + dec * dot_nt(mine, ub[rows])
            dus.append(du)
        ubf = ub.astype(f32)
        dyf = dyb.astype(f32)
        net = jnp.concatenate(
            [
                dyf[:SPAN] * y_r[:SPAN, at] - ubf[:SPAN] * dus[0] - kept.astype(f32) * under,
                dyf[SPAN:] * (y_r[SPAN:, at] - ge * over) + zb.astype(f32) * over
                - ubf[SPAN:] * dus[1],
            ],
            0,
        )
        du = jnp.concatenate([dus[0] + ce * under, dus[1]], 0)
        fold = (fold_col == j * per + fold_row // width).astype(bf16)
        dcum = dcum + dot_nn(halves(net), fold)
        dstep = dstep + dot_nn(halves(du * xs), fold)
        skip = jnp.broadcast_to(jnp.sum(dy * xs, axis=0, keepdims=True), (8, LANES))
        dskip = dskip + dot_nn(halves(skip), fold)
        dxc = (du * se + dsk[:, at] * dy) * silu_slope(xc)
        dpre, dw, db = conv_back(dxc, xpre_r[:, at], cx[:, at], lk)
        dx_o[:, at] = dpre.astype(bf16)
        for k, piece in enumerate(dw):
            sm_o[k : k + 1, at] = piece
        sm_o[4:5, at] = db
    upper = (iota((rows_t, rows_t), 0) <= iota((rows_t, rows_t), 1)) & (segc[...] == segr[...])
    dlog = dot_nn(upper.astype(f32), dcum, HI)
    ddt = (dstep - dlog * jnp.exp(alog[...])) * jax.nn.sigmoid(v)
    dx_o[:, inner + 2 * state :] = ddt.astype(bf16)
    sm_o[7:8, :LANES] = jnp.sum(ddt, axis=0, keepdims=True)
    sm_o[7:8, LANES : 2 * LANES] = jnp.sum(dlog * logd, axis=0, keepdims=True)
    sm_o[7:8, 2 * LANES : 3 * LANES] = dskip[:1]
    for k in range(2):
        rows = slice(k * SPAN, (k + 1) * SPAN)
        db = dot_tn(dsc[k], cs[rows], HI)
        dc = dot_nn(dsc[k], bs[rows], HI)
        if k == 0:
            db = db + db0
        else:
            dc = dc + dc1
        dc_s[rows, :state] = db
        dc_s[rows, state:] = dc
    for c in range(2 * state // LANES):
        at = slice(c * LANES, (c + 1) * LANES)
        dpre, dw, db = conv_back(
            dc_s[:, at] * silu_slope(bcc_r[:, at]), bcpre_r[:, at], cbc[:, at], lk
        )
        dx_o[:, inner + c * LANES : inner + (c + 1) * LANES] = dpre.astype(bf16)
        for k, piece in enumerate(dw):
            sm_o[8 + k : 9 + k, at] = piece
        sm_o[12:13, at] = db
    wide = keep_o.shape[1]
    half = keep_o.shape[0]
    for first in range(0, wide, 2 * LANES):
        at = slice(first, min(first + 2 * LANES, wide))
        send_o[:, at] = dot_nn(nrm_t[half:], dx_o[:, at]).astype(bf16)
        keep_o[:, at] = dot_nn(nrm_t[:half], dx_o[:, at]).astype(bf16)


def dn_body(side, dz, wza, wzb, dx, w1a, w1b, own_o, other_o, all_s):
    half = wza.shape[0]
    count = own_o.shape[0]
    a = dz[...]
    b = dx[...]
    all_s[:, :half] = dot_nt(a, wza[...]) + dot_nt(b, w1a[...])
    all_s[:, half:] = dot_nt(a, wzb[...]) + dot_nt(b, w1b[...])
    other_o[...] = all_s[rows_of(1 - side[0], count), :].astype(bf16)
    own_o[...] = all_s[rows_of(side[0], count), :]


def last_body(side, keep, other, x_o, dt_o, own_o, send_o, all_s):
    inner = x_o.shape[1]
    count, two_state = own_o.shape
    x_o[...] = keep[:, :inner].astype(f32) + other[:, :inner].astype(f32)
    all_s[...] = keep[:, inner:].astype(f32) + other[:, inner:].astype(f32)
    dt_o[...] = all_s[:, two_state : two_state + dt_o.shape[1]]
    low = all_s[:count, :two_state]
    top = all_s[count:, :two_state]
    own_o[...] = jnp.where(side[0] == 0, low, top)
    send_o[...] = jnp.where(side[0] == 0, top, low)


def restore(v, place_t):
    both = dot_nn(split(v), place_t)
    return both[: v.shape[0]] + both[v.shape[0] :]


def block_body(res, own, other, place, out_o):
    out_o[...] = res[...] + restore(own[...] + other[...].astype(f32), place[...])


def tail_body(res, cot, gain, own, other, place, ig_o, np_o):
    r = res[...]
    dn = restore(own[...] + other[...].astype(f32), place[...])
    inv = lax.rsqrt(jnp.mean(r * r, axis=1, keepdims=True) + epsilon)
    np_o[...] = jnp.sum(dn * r * inv, axis=0, keepdims=True)
    dg = dn * gain[...]
    inner = jnp.sum(dg * r, axis=1, keepdims=True) / r.shape[1]
    ig_o[...] = cot[...] + inv * dg - r * (inv * inv * inv * inner)


def join_body(side, own, other, all_o, turned_o):
    half = own.shape[0]
    all_o[rows_of(side[0], half), :] = own[...]
    all_o[rows_of(1 - side[0], half), :] = other[...]
    turned_o[...] = all_o[...].T


def cat_body(first, second, out_o):
    half = first.shape[0]
    out_o[:half] = first[...]
    out_o[half:] = second[...]


def head_body(res, cot, gain, place, nrm_o, cot_o):
    r = res[...]
    inv = lax.rsqrt(jnp.mean(r * r, axis=1, keepdims=True) + epsilon)
    n = (r * inv * gain[...]).astype(bf16)
    nrm_o[...] = dot_nn(n, place[...]).astype(bf16)
    cot_o[...] = dot_nn(cot[...].astype(bf16), place[...]).astype(bf16)


def solution(mesh):
    n = mesh.shape["dp"]
    nt = mesh.shape["tensor"]
    bits = [1 << k for k in range(n.bit_length() - 1)]
    assert (1 << len(bits)) == n and nt == 2

    def swap(v, bit):
        return lax.ppermute(v, "dp", [(i, i ^ bit) for i in range(n)])

    def cross(v):
        return lax.ppermute(v, "tensor", [(0, 1), (1, 0)])

    def after(v, *others):
        return lax.optimization_barrier((v,) + others)[0]

    def gather(v, start):
        if start is not None:
            v = after(v, start)
        marks = []
        for bit in reversed(bits):
            r = swap(v, bit)
            marks.append(r)
            if bit > 1:
                (v,) = call(0.5, cat_body, [((2 * v.shape[0], v.shape[1]), bf16)], v, r)
        return v, r, marks

    def plus(a, b):
        return a.astype(f32) + b.astype(f32)

    near = list(range(1, len(bits)))

    far = near[1:] + near[:1]

    def scatter(keep, send, order):
        shape = (2,) * (len(bits) - 1) + (keep.shape[0] >> (len(bits) - 1), keep.shape[1])
        left = list(near)
        keep = keep.reshape(shape)
        r = swap(send, bits[0]).reshape(shape)
        for which in order:
            axis = left.index(which)
            left.pop(axis)
            pick = [[lax.index_in_dim(v, side, axis, False) for v in (keep, r)] for side in (0, 1)]
            send = plus(*pick[1]).astype(bf16)
            keep = plus(*pick[0]).astype(bf16)
            flat = send.reshape(-1, send.shape[-1])
            r = swap(flat, bits[which]).reshape(send.shape)
        return keep, r

    def whole(residual, segment_ids, live_counts, norm_gain, z_weight, x_weight, bc_weight,
              dt_weight, conv_x, conv_x_bias, conv_bc, conv_bc_bias, dt_bias, a_log, d_skip,
              gate_gain, out_weight, cotangent):
        half, width_d = residual.shape
        tokens = segment_ids.shape[0]
        inner = x_weight.shape[1]
        heads = dt_weight.shape[1]
        two_state = bc_weight.shape[1]
        head_width = inner // heads
        full = float(inner * nt)
        shard = width_d // n
        me = lax.axis_index("dp")
        side = lax.axis_index("tensor")

        pad = LANES - heads
        w1s = jnp.concatenate([x_weight, bc_weight, jnp.pad(dt_weight, ((0, 0), (0, pad)))], 1)
        outa, outb, m1 = gather(out_weight.T, None)
        w1a, w1b, m2 = gather(w1s, m1[0])
        wza, wzb, _ = gather(z_weight, m2[0])

        spot = jnp.arange(width_d, dtype=jnp.int32)
        block = spot // shard
        turned = jnp.zeros_like(block)
        for k in range(len(bits)):
            turned = turned | (((block >> k) & 1) << (len(bits) - 1 - k))
        source = (turned ^ me) * shard + spot % shard
        place = (spot[:, None] == source[None, :]).astype(bf16)
        place_t = (source[:, None] == spot[None, :]).astype(bf16)

        spots = jnp.arange(tokens)
        links = [jnp.ones((tokens,), f32)]
        for lag in range(1, conv_x.shape[0]):
            moved = jnp.concatenate(
                [jnp.full((lag,), -1, jnp.int32), segment_ids[: tokens - lag]]
            )
            links.append((segment_ids == moved).astype(f32))
        link = jnp.stack(links, 1)
        segc = segment_ids[:, None]
        segr = segment_ids[None, :]
        live = (spots < live_counts[0]).astype(f32)[:, None]
        dtb = jnp.pad(dt_bias, (0, pad))[None, :]
        alog = jnp.pad(a_log, (0, pad))[None, :]
        dsk = jnp.repeat(d_skip, head_width)[None, :]
        gain = norm_gain[None, :]
        gg = gate_gain[None, :]
        cxb = conv_x_bias[None, :]
        cbcb = conv_bc_bias[None, :]
        where = side.astype(jnp.int32)[None]
        (residual, link, segc, segr, live, dtb, alog, dsk, gain, gg, cxb, cbcb, where, place,
         place_t) = lax.optimization_barrier(
            (residual, link, segc, segr, live, dtb, alog, dsk, gain, gg, cxb, cbcb, where, place,
             place_t)
        )
        nrm_half, cot_half = call(
            1.5, head_body, [((half, width_d), bf16)] * 2, residual, cotangent, gain, place
        )
        joined = [((tokens, width_d), bf16), ((width_d, tokens), bf16)]
        nrm_other = cross(nrm_half)
        nrm, nrm_t = call(1.0, join_body, joined, where, nrm_half, nrm_other, scalars=1)
        cot_other = cross(cot_half)
        cot, cot_t = call(1.0, join_body, joined, where, cot_half, cot_other, scalars=1)

        big = ((tokens, inner), f32)

        def fwd(*a):
            return fwd_body(head_width, *a)

        (dm,) = call(3.0, dmix_body, [big], cot, outa, outb, live)
        xpre, xc, y, bcpre, bcc, dtp, dec = call(
            7.0, fwd,
            [big, big, big, ((tokens, two_state), f32), ((tokens, two_state), f32),
             ((tokens, LANES), f32), ((2 * heads, SPAN, SPAN), f32)],
            nrm, w1a, w1b, link, segc, segr, conv_x, cxb, conv_bc, cbcb, dtb, alog,
        )
        z, g, sums = call(
            5.0, gate_body, [big, big, ((16, tokens), f32)],
            nrm, wza, wzb, y, xc, dsk, dm, gg,
        )
        sums2 = cross(sums)

        def mix(*a):
            return mix_body(full, *a)

        cut = width_d // 2
        apart = [((half, width_d), f32), ((half, width_d), bf16)]
        out_keep, out_send, mixed = call(
            4.0, mix,
            [((cut, inner), bf16), ((cut, inner), bf16), ((tokens, inner), bf16)],
            g, sums, sums2, gg, live, cot_t,
        )
        blk_own, blk_send = call(2.5, blk_body, apart, where, mixed, outa, outb, scalars=1)
        out_sum = plus(*scatter(out_keep, out_send, near))

        blk_other = cross(blk_send)
        (block_out,) = call(
            2.5, block_body, [((half, width_d), f32)], residual, blk_own, blk_other, place_t
        )

        def back_z(*a):
            return dz_body(full, *a)

        dz, dy, gain_part, z_keep, z_send = call(
            6.0, back_z,
            [((tokens, inner), bf16), big, ((1, inner), f32), ((cut, inner), bf16),
             ((cut, inner), bf16)],
            after(nrm_t, out_send), g, dm, z, y, xc, dsk, gg, sums, sums2,
        )
        z_weight_grad = plus(*scatter(z_keep, z_send, far))

        def back(*a):
            return bwd_body(head_width, *a)

        wide = w1a.shape[1]
        dx, small, x_keep, x_send = call(
            14.0, back,
            [((tokens, wide), bf16), ((16, inner), f32), ((cut, wide), bf16), ((cut, wide), bf16)],
            nrm_t, dy, xpre, xc, y, bcpre, bcc, dtp, dec, link, segc, segr, conv_x, conv_bc, dtb, alog,
            dsk,
            scratch=[pltpu.VMEM((tokens, two_state), f32)],
        )
        x_weight_grad, dt_weight_grad, bc_own, bc_send = call(
            1.5, last_body,
            [((shard, inner), f32), ((shard, heads), f32)] + [((shard // nt, two_state), f32)] * 2,
            where, *scatter(x_keep, x_send, near), scalars=1,
            scratch=[pltpu.VMEM((shard, wide - inner), f32)],
        )
        bc_weight_grad = bc_own + cross(bc_send)

        dn_own, dn_send = call(
            5.0, dn_body, apart, where, dz, wza, wzb, dx, w1a, w1b, scalars=1,
            scratch=[pltpu.VMEM((tokens, width_d), f32)],
        )
        dn_other = cross(dn_send)
        input_grad, norm_part = call(
            4.0, tail_body, [((half, width_d), f32), ((1, width_d), f32)],
            residual, cotangent, gain, dn_own, dn_other, place_t,
        )

        few = jnp.concatenate(
            [small[:5], gain_part, small[6:13], norm_part], 0
        )
        few = jnp.concatenate([few[:8], few[13:14], few[8:13], few[:2]], 0)
        for bit in bits:
            few = few + swap(few, bit)
        shared = few[8:16]
        shared = shared + cross(shared)
        return (
            block_out,
            input_grad,
            shared[0],
            z_weight_grad,
            x_weight_grad,
            bc_weight_grad,
            dt_weight_grad,
            few[:4],
            few[4],
            shared[1:5, :two_state],
            shared[5, :two_state],
            few[7, :heads],
            few[7, LANES : LANES + heads],
            few[7, 2 * LANES : 2 * LANES + heads],
            few[5],
            out_sum.T,
        )

    placed = (
        P(("dp", "tensor"), None),
        P("dp"),
        P("dp"),
        P(),
        P("dp", "tensor"),
        P("dp", "tensor"),
        P("dp", None),
        P("dp", "tensor"),
        P(None, "tensor"),
        P("tensor"),
        P(),
        P(),
        P("tensor"),
        P("tensor"),
        P("tensor"),
        P("tensor"),
        P("tensor", "dp"),
        P(("dp", "tensor"), None),
    )

    return jax.shard_map(
        whole,
        mesh=mesh,
        in_specs=placed,
        out_specs=(
            P(("dp", "tensor"), None),
            P(("dp", "tensor"), None),
            P(),
            P("dp", "tensor"),
            P("dp", "tensor"),
            P(("dp", "tensor"), None),
            P("dp", "tensor"),
            P(None, "tensor"),
            P("tensor"),
            P(),
            P(),
            P("tensor"),
            P("tensor"),
            P("tensor"),
            P("tensor"),
            P("tensor", "dp"),
        ),
        check_vma=False,
    )
```

```python
import jax
import jax.numpy as jnp
from jax import lax
from jax.experimental import pallas as pl
from jax.experimental.pallas import tpu as pltpu
from jax.sharding import PartitionSpec as P


SPAN = 128
LANES = 128
VMEM = 20 * 1024 * 1024
epsilon = 1e-05
f32 = jnp.float32
bf16 = jnp.bfloat16
HI = lax.Precision.HIGHEST


def dot_nn(a, b, p=None):
    return lax.dot_general(a, b, (((1,), (0,)), ((), ())), precision=p, preferred_element_type=f32)


def dot_nt(a, b, p=None):
    return lax.dot_general(a, b, (((1,), (1,)), ((), ())), precision=p, preferred_element_type=f32)


def dot_tn(a, b, p=None):
    return lax.dot_general(a, b, (((0,), (0,)), ((), ())), precision=p, preferred_element_type=f32)


def call(micros, body, outs, *args, scratch=(), scalars=0):
    return pl.pallas_call(
        body,
        out_shape=[jax.ShapeDtypeStruct(s, d) for s, d in outs],
        in_specs=[pl.BlockSpec(memory_space=pltpu.SMEM)] * scalars
        + [pl.BlockSpec(memory_space=pltpu.VMEM)] * (len(args) - scalars),
        scratch_shapes=list(scratch),
        cost_estimate=pl.CostEstimate(
            flops=int(micros * 9e8), transcendentals=0, bytes_accessed=int(micros * 3e6)
        ),
        compiler_params=pltpu.CompilerParams(vmem_limit_bytes=VMEM),
    )(*args)


def paired(a, w, at):
    half = w[0].shape[0]
    return dot_nn(a[:, :half], w[0][:, at]) + dot_nn(a[:, half:], w[1][:, at])


def split(v):
    high = v.astype(bf16)
    return jnp.concatenate([high, (v - high.astype(f32)).astype(bf16)], 0)


def halves(v):
    high = v.astype(bf16)
    return jnp.concatenate([high, (v - high.astype(f32)).astype(bf16)], 1)


def rows_of(side, half):
    return pl.ds(pl.multiple_of(side * half, half), half)


def iota(shape, axis):
    return lax.broadcasted_iota(jnp.int32, shape, axis)


def silu(v):
    return v * jax.nn.sigmoid(v)


def silu_slope(v):
    s = jax.nn.sigmoid(v)
    return s * (1.0 + v * (1.0 - s))


def conv(v, w, b, link):
    taps = w.shape[0]
    out = b + w[taps - 1 : taps] * v
    for lag in range(1, taps):
        moved = pltpu.roll(v, lag, 0) * link[:, lag : lag + 1]
        out = out + w[taps - 1 - lag : taps - lag] * moved
    return out


def conv_back(dv, v, w, link):
    taps = w.shape[0]
    rows = v.shape[0]
    dpre = w[taps - 1 : taps] * dv
    dw = [jnp.sum(dv * v, axis=0, keepdims=True)]
    for lag in range(1, taps):
        masked = dv * link[:, lag : lag + 1]
        dw.insert(0, jnp.sum(masked * pltpu.roll(v, lag, 0), axis=0, keepdims=True))
        dpre = dpre + w[taps - 1 - lag : taps - lag] * pltpu.roll(masked, rows - lag, 0)
    return dpre, dw, jnp.sum(dv, axis=0, keepdims=True)


def prepare(dtpre, dtb, alog, segc, segr):
    v = dtpre + dtb
    step = jnp.maximum(v, 0.0) + jnp.log1p(jnp.exp(-jnp.abs(v)))
    logd = -step * jnp.exp(alog)
    row = iota((SPAN, SPAN), 0)
    col = iota((SPAN, SPAN), 1)
    lower = row >= col
    tri = lower.astype(f32)
    cum = [dot_nn(tri, logd[k * SPAN : (k + 1) * SPAN], HI) for k in range(2)]
    cum_t = [c.T for c in cum]
    mask = [
        (segc[k * SPAN : (k + 1) * SPAN] == segr[:, k * SPAN : (k + 1) * SPAN]) & lower
        for k in range(2)
    ]
    edge = segc[SPAN - 1 : SPAN]
    keep = (segc[SPAN:] == edge).astype(f32)
    tail = (segc[:SPAN] == edge).astype(f32)
    grow = jnp.exp(cum[1]) * keep
    coef = jnp.exp(cum[0][SPAN - 1 : SPAN] - cum[0]) * tail
    return v, step, logd, cum, cum_t, mask, grow, coef


def spread(v, first, width):
    lane = iota((v.shape[0], LANES), 1)
    out = jnp.broadcast_to(v[:, first : first + 1], (v.shape[0], LANES))
    for k in range(1, LANES // width):
        out = jnp.where(lane >= k * width, v[:, first + k : first + k + 1], out)
    return out


def decay(cum, cum_t, mask, h):
    return jnp.where(mask, jnp.exp(cum[:, h : h + 1] - cum_t[h : h + 1, :]), 0.0)


def fwd_body(width, nrm, w1a, w1b, cols, segr, cx, cxb, cbc, cbcb, dtb, alog,
             xpre_o, xc_o, y_o, bcpre_o, bcc_o, dt_o, dec_o):
    inner = xc_o.shape[1]
    state = bcc_o.shape[1] // 2
    x = nrm[...]
    w1 = (w1a, w1b)
    pre = paired(x, w1, slice(inner, w1a.shape[1]))
    bcpre_o[...] = pre[:, : 2 * state]
    dt_o[...] = pre[:, 2 * state :]
    wide = 2 * LANES
    for c in range(inner // wide):
        xpre_o[:, c * wide : (c + 1) * wide] = paired(x, w1, slice(c * wide, (c + 1) * wide))
    lk = cols[:, :SEG]
    for c in range(2 * state // LANES):
        at = slice(c * LANES, (c + 1) * LANES)
        bcc_o[:, at] = conv(bcpre_o[:, at], cbc[:, at], cbcb[:, at], lk)
    bs = silu(bcc_o[:, :state])
    cs = silu(bcc_o[:, state:])
    _, step, _, cum, cum_t, mask, grow, coef = prepare(
        dt_o[...], dtb[...], alog[...], cols[:, SEG : SEG + 1], segr[...]
    )
    scores = [
        dot_nt(cs[k * SPAN : (k + 1) * SPAN], bs[k * SPAN : (k + 1) * SPAN], HI) for k in range(2)
    ]
    b0 = bs[:SPAN].astype(bf16)
    c1 = cs[SPAN:].astype(bf16)
    c1 = jnp.concatenate([c1, c1], 1)
    per = LANES // width
    lane = iota((SPAN, LANES), 1)
    for j in range(inner // LANES):
        at = slice(j * LANES, (j + 1) * LANES)
        xc = conv(xpre_o[:, at], cx[:, at], cxb[:, at], lk)
        xc_o[:, at] = xc
        u = spread(step, j * per, width) * silu(xc)
        ub = u.astype(bf16)
        for k in range(2):
            rows = slice(k * SPAN, (k + 1) * SPAN)
            y = None
            for i in range(per):
                h = j * per + i
                dec = decay(cum[k], cum_t[k], mask[k], h)
                dec_o[2 * h + k] = dec
                w = (dec * scores[k]).astype(bf16)
                part = dot_nn(w, ub[rows])
                y = part if y is None else jnp.where(lane >= i * width, part, y)
            if k:
                kept = (spread(coef, j * per, width) * u[:SPAN]).astype(bf16)
                st = split(dot_tn(b0, kept))
                y = y + spread(grow, j * per, width) * dot_nn(c1, st)
            y_o[rows, at] = y


def as_rows(col):
    return jnp.broadcast_to(col, (col.shape[0], LANES)).T[:8]


def as_col(rows):
    return jnp.broadcast_to(rows[:1], (LANES, rows.shape[1])).T[:, :1]


def dmix_body(cot, outa, outb, cols, dm_o):
    wide = 2 * LANES
    x = cot[...]
    lv = cols[:, LIVE : LIVE + 1]
    for c in range(dm_o.shape[1] // wide):
        at = slice(c * wide, (c + 1) * wide)
        dm_o[:, at] = paired(x, (outa, outb), at) * lv


def gate_body(nrm, wza, wzb, y_r, xc_r, dsk, dm_r, gain, z_o, g_o, sums_o):
    wide = 2 * LANES
    x = nrm[...]
    squares = jnp.zeros((x.shape[0], LANES), f32)
    dots = jnp.zeros((x.shape[0], LANES), f32)
    for c in range(z_o.shape[1] // wide):
        at = slice(c * wide, (c + 1) * wide)
        z_o[:, at] = paired(x, (wza, wzb), at)
    for c in range(z_o.shape[1] // LANES):
        at = slice(c * LANES, (c + 1) * LANES)
        g = (y_r[:, at] + dsk[:, at] * silu(xc_r[:, at])) * silu(z_o[:, at])
        g_o[:, at] = g
        squares = squares + g * g
        dots = dots + dm_r[:, at] * gain[:, at] * g
    sums_o[:8] = as_rows(jnp.sum(squares, axis=1, keepdims=True))
    sums_o[8:] = as_rows(jnp.sum(dots, axis=1, keepdims=True))


def mix_body(full, g_r, sums, sums2, gain, cols, cot_t, keep_o, send_o, mixed):
    inv = lax.rsqrt(as_col(sums[:8] + sums2[:8]) / full + epsilon)
    wide = 2 * LANES
    for c in range(g_r.shape[1] // LANES):
        at = slice(c * LANES, (c + 1) * LANES)
        mixed[:, at] = (g_r[:, at] * inv * gain[:, at] * cols[:, LIVE : LIVE + 1]).astype(bf16)
    half = keep_o.shape[0]
    for c in range(g_r.shape[1] // wide):
        at = slice(c * wide, (c + 1) * wide)
        send_o[:, at] = dot_nn(cot_t[half:], mixed[:, at]).astype(bf16)
        keep_o[:, at] = dot_nn(cot_t[:half], mixed[:, at]).astype(bf16)


def blk_body(side, mixed, outa, outb, own_o, other_o):
    half = outa.shape[0]
    count = own_o.shape[0]
    m = mixed[rows_of(1 - side[0], count), :]
    other_o[:, :half] = dot_nt(m, outa[...]).astype(bf16)
    other_o[:, half:] = dot_nt(m, outb[...]).astype(bf16)
    m = mixed[rows_of(side[0], count), :]
    own_o[:, :half] = dot_nt(m, outa[...])
    own_o[:, half:] = dot_nt(m, outb[...])


def dz_body(full, nrm_t, g_r, dm_r, z_r, y_r, xc_r, dsk, gain, sums, sums2,
            dz_o, dy_o, gp_o, keep_o, send_o):
    inv = lax.rsqrt(as_col(sums[:8] + sums2[:8]) / full + epsilon)
    back = inv * inv * inv * as_col(sums[8:] + sums2[8:]) / full
    for c in range(z_r.shape[1] // LANES):
        at = slice(c * LANES, (c + 1) * LANES)
        z = z_r[:, at]
        s = jax.nn.sigmoid(z)
        g = g_r[:, at]
        dm = dm_r[:, at]
        gp_o[:, at] = jnp.sum(dm * g * inv, axis=0, keepdims=True)
        dg = inv * (dm * gain[:, at]) - g * back
        y = y_r[:, at] + dsk[:, at] * silu(xc_r[:, at])
        dz_o[:, at] = (dg * y * (s * (1.0 + z * (1.0 - s)))).astype(bf16)
        dy_o[:, at] = dg * (z * s)
    half = keep_o.shape[0]
    wide = 2 * LANES
    for c in range(z_r.shape[1] // wide):
        at = slice(c * wide, (c + 1) * wide)
        send_o[:, at] = dot_nn(nrm_t[half:], dz_o[:, at]).astype(bf16)
        keep_o[:, at] = dot_nn(nrm_t[:half], dz_o[:, at]).astype(bf16)


def bwd_body(width, nrm_t, dy_r, xpre_r, xc_r, y_r, bcpre_r, bcc_r, dt_r, dec_r, cols, segr, cx,
             cbc, dtb, alog, dsk, dx_o, dbc_o, sm_o, keep_o, send_o, dc_s):
    inner = xc_r.shape[1]
    state = bcc_r.shape[1] // 2
    lk = cols[:, :SEG]
    segc = cols[:, SEG : SEG + 1]
    bs = silu(bcc_r[:, :state])
    cs = silu(bcc_r[:, state:])
    v, step, logd, _, _, _, grow, coef = prepare(dt_r[...], dtb[...], alog[...], segc, segr[...])
    scores = [
        dot_nt(cs[k * SPAN : (k + 1) * SPAN], bs[k * SPAN : (k + 1) * SPAN], HI) for k in range(2)
    ]
    b0 = bs[:SPAN].astype(bf16)
    c1 = cs[SPAN:].astype(bf16)
    b00 = jnp.concatenate([b0, b0], 1)
    c11 = jnp.concatenate([c1, c1], 1)
    per = LANES // width
    lane = iota((SPAN, LANES), 1)
    rows_t = 2 * SPAN
    dcum = jnp.zeros((rows_t, LANES), f32)
    dstep = jnp.zeros((rows_t, LANES), f32)
    dskip = jnp.zeros((8, LANES), f32)
    dsc = [jnp.zeros((SPAN, SPAN), f32) for _ in range(2)]
    dc1 = jnp.zeros((SPAN, state), f32)
    db0 = jnp.zeros((SPAN, state), f32)
    fold_row = iota((2 * LANES, LANES), 0) % LANES
    fold_col = iota((2 * LANES, LANES), 1)
    sm_o[...] = jnp.zeros(sm_o.shape, f32)
    for j in range(inner // LANES):
        at = slice(j * LANES, (j + 1) * LANES)
        xc = xc_r[:, at]
        xs = silu(xc)
        se = spread(step, j * per, width)
        u = se * xs
        ub = u.astype(bf16)
        dy = dy_r[:, at]
        dyb = dy.astype(bf16)
        ce = spread(coef, j * per, width)
        ge = spread(grow, j * per, width)
        kept = (ce * u[:SPAN]).astype(bf16)
        st = split(dot_tn(b0, kept))
        zb = (ge * dy[SPAN:]).astype(bf16)
        dst = split(dot_tn(c1, zb))
        dc1 = dc1 + dot_nt(zb, st[:state])
        db0 = db0 + dot_nt(kept, dst[:state])
        over = dot_nn(c11, st)
        under = dot_nn(b00, dst)
        dus = []
        for k in range(2):
            rows = slice(k * SPAN, (k + 1) * SPAN)
            du = None
            for i in range(per):
                h = j * per + i
                dec = dec_r[2 * h + k]
                w = (dec * scores[k]).astype(bf16)
                part = dot_tn(w, dyb[rows])
                du = part if du is None else jnp.where(lane >= i * width, part, du)
                inside = (lane >= i * width) & (lane < (i + 1) * width)
                mine = jnp.where(inside, dy[rows], 0.0).astype(bf16)
                dsc[k] = dsc[k] + dec * dot_nt(mine, ub[rows])
            dus.append(du)
        ubf = ub.astype(f32)
        dyf = dyb.astype(f32)
        net = jnp.concatenate(
            [
                dyf[:SPAN] * y_r[:SPAN, at] - ubf[:SPAN] * dus[0] - kept.astype(f32) * under,
                dyf[SPAN:] * (y_r[SPAN:, at] - ge * over) + zb.astype(f32) * over
                - ubf[SPAN:] * dus[1],
            ],
            0,
        )
        du = jnp.concatenate([dus[0] + ce * under, dus[1]], 0)
        fold = (fold_col == j * per + fold_row // width).astype(bf16)
        dcum = dcum + dot_nn(halves(net), fold)
        dstep = dstep + dot_nn(halves(du * xs), fold)
        skip = jnp.broadcast_to(jnp.sum(dy * xs, axis=0, keepdims=True), (8, LANES))
        dskip = dskip + dot_nn(halves(skip), fold)
        dxc = (du * se + dsk[:, at] * dy) * silu_slope(xc)
        dpre, dw, db = conv_back(dxc, xpre_r[:, at], cx[:, at], lk)
        dx_o[:, at] = dpre.astype(bf16)
        for k, piece in enumerate(dw):
            sm_o[k : k + 1, at] = piece
        sm_o[4:5, at] = db
    upper = (iota((rows_t, rows_t), 0) <= iota((rows_t, rows_t), 1)) & (segc == segr[...])
    dlog = dot_nn(upper.astype(f32), dcum, HI)
    ddt = (dstep - dlog * jnp.exp(alog[...])) * jax.nn.sigmoid(v)
    dx_o[:, inner + 2 * state :] = ddt.astype(bf16)
    sm_o[7:8, :LANES] = jnp.sum(ddt, axis=0, keepdims=True)
    sm_o[7:8, LANES : 2 * LANES] = jnp.sum(dlog * logd, axis=0, keepdims=True)
    sm_o[7:8, 2 * LANES : 3 * LANES] = dskip[:1]
    for k in range(2):
        rows = slice(k * SPAN, (k + 1) * SPAN)
        db = dot_tn(dsc[k], cs[rows], HI)
        dc = dot_nn(dsc[k], bs[rows], HI)
        if k == 0:
            db = db + db0
        else:
            dc = dc + dc1
        dc_s[rows, :state] = db
        dc_s[rows, state:] = dc
    for c in range(2 * state // LANES):
        at = slice(c * LANES, (c + 1) * LANES)
        dpre, dw, db = conv_back(
            dc_s[:, at] * silu_slope(bcc_r[:, at]), bcpre_r[:, at], cbc[:, at], lk
        )
        dx_o[:, inner + c * LANES : inner + (c + 1) * LANES] = dpre.astype(bf16)
        dbc_o[:, at] = dpre.astype(bf16)
        for k, piece in enumerate(dw):
            sm_o[8 + k : 9 + k, at] = piece
        sm_o[12:13, at] = db
    wide = keep_o.shape[1]
    half = keep_o.shape[0]
    for first in range(0, wide, 2 * LANES):
        at = slice(first, min(first + 2 * LANES, wide))
        send_o[:, at] = dot_nn(nrm_t[half:], dx_o[:, at]).astype(bf16)
        keep_o[:, at] = dot_nn(nrm_t[:half], dx_o[:, at]).astype(bf16)


def dn_body(side, dz, wza, wzb, dx, w1a, w1b, own_o, other_o, all_s):
    half = wza.shape[0]
    count = own_o.shape[0]
    a = dz[...]
    b = dx[...]
    all_s[:, :half] = dot_nt(a, wza[...]) + dot_nt(b, w1a[...])
    all_s[:, half:] = dot_nt(a, wzb[...]) + dot_nt(b, w1b[...])
    other_o[...] = all_s[rows_of(1 - side[0], count), :].astype(bf16)
    own_o[...] = all_s[rows_of(side[0], count), :]


def last_body(keep, other, bc_o, dt_o):
    two_state = bc_o.shape[1]
    count, heads = keep.shape[0], dt_o.shape[1]
    bc_o[...] = keep[:, :two_state].astype(f32) + other[:, :two_state].astype(f32)
    dt = keep[:, two_state:].astype(f32) + other[:, two_state:].astype(f32)
    dt_o[:count] = dt[:, :heads]
    dt_o[count:] = pltpu.roll(dt, LANES // 2, 1)[:, :heads]


def few_body(few, other, norm_o, x_o, xb_o, bc_o, bcb_o, gain_o, heads_o):
    taps = x_o.shape[0]
    width = bc_o.shape[1]
    shared = few[8:16] + other[...]
    norm_o[...] = shared[:1]
    bc_o[...] = shared[1 : 1 + taps, :width]
    bcb_o[...] = shared[1 + taps : 2 + taps, :width]
    x_o[...] = few[:taps]
    xb_o[...] = few[taps : taps + 1]
    gain_o[...] = few[5:6]
    heads_o[...] = few[7:8, : 3 * LANES]


def restore(v, place_t):
    both = dot_nn(split(v), place_t)
    return both[: v.shape[0]] + both[v.shape[0] :]


def block_body(res, own, other, place, out_o):
    out_o[...] = res[...] + restore(own[...] + other[...].astype(f32), place[...])


def tail_body(res, cot, gain, own, other, place, ig_o, np_o):
    r = res[...]
    dn = restore(own[...] + other[...].astype(f32), place[...])
    inv = lax.rsqrt(jnp.mean(r * r, axis=1, keepdims=True) + epsilon)
    np_o[...] = jnp.sum(dn * r * inv, axis=0, keepdims=True)
    dg = dn * gain[...]
    inner = jnp.sum(dg * r, axis=1, keepdims=True) / r.shape[1]
    ig_o[...] = cot[...] + inv * dg - r * (inv * inv * inv * inner)


SEG = 4
LIVE = 5


def prep_body(taps, count, segr, cols_o):
    tokens = segr.shape[1]
    seg = jnp.broadcast_to(segr[...], (LANES, tokens)).T
    row = iota(seg.shape, 0)
    lane = iota(seg.shape, 1)
    out = jnp.where(lane == SEG, seg, 0.0)
    out = jnp.where((lane == LIVE) & (row < count[0]), 1.0, out)
    for lag in range(taps):
        moved = pltpu.roll(seg, lag, 0) if lag else seg
        out = jnp.where((lane == lag) & (row >= lag) & (seg == moved), 1.0, out)
    cols_o[...] = out


def join_body(side, own, other, all_o, turned_o):
    half = own.shape[0]
    all_o[rows_of(side[0], half), :] = own[...]
    all_o[rows_of(1 - side[0], half), :] = other[...]
    turned_o[...] = all_o[...].T


def order_body(turned, picks, halves_o):
    halves_o[...] = dot_nn(picks[...], turned[...]).astype(bf16)


def bpart_body(side, ordered, dx, theirs, keep_o, send_o):
    two_state = theirs.shape[1]
    inner = dx.shape[1] - two_state - LANES
    count = keep_o.shape[0]
    whole = 2 * count
    rows = ordered[rows_of(side[0], whole), :]
    own = dot_nn(rows, dx[:, inner : inner + two_state]) + dot_nn(rows, theirs[...])
    lane = iota((whole, LANES), 1)
    ddt = dx[:, inner + two_state :]
    first = dot_nn(ordered[:whole], ddt)
    second = dot_nn(ordered[whole:], ddt)
    dt = jnp.where(lane < LANES // 2, first, pltpu.roll(second, LANES // 2, 1))
    for out, at in ((keep_o, slice(0, count)), (send_o, slice(count, whole))):
        out[:, :two_state] = own[at].astype(bf16)
        out[:, two_state:] = dt[at].astype(bf16)


def cat_body(first, second, out_o):
    half = first.shape[0]
    out_o[:half] = first[...]
    out_o[half:] = second[...]


def head_body(res, cot, gain, place, nrm_o, cot_o):
    r = res[...]
    inv = lax.rsqrt(jnp.mean(r * r, axis=1, keepdims=True) + epsilon)
    n = (r * inv * gain[...]).astype(bf16)
    nrm_o[...] = dot_nn(n, place[...]).astype(bf16)
    cot_o[...] = dot_nn(cot[...].astype(bf16), place[...]).astype(bf16)


def solution(mesh):
    n = mesh.shape["dp"]
    nt = mesh.shape["tensor"]
    bits = [1 << k for k in range(n.bit_length() - 1)]
    assert (1 << len(bits)) == n and nt == 2

    def swap(v, bit):
        return lax.ppermute(v, "dp", [(i, i ^ bit) for i in range(n)])

    def cross(v):
        return lax.ppermute(v, "tensor", [(0, 1), (1, 0)])

    def after(v, *others):
        return lax.optimization_barrier((v,) + others)[0]

    def gather(v, start):
        if start is not None:
            v = after(v, start)
        marks = []
        for bit in reversed(bits):
            r = swap(v, bit)
            marks.append(r)
            if bit > 1:
                (v,) = call(0.5, cat_body, [((2 * v.shape[0], v.shape[1]), bf16)], v, r)
        return v, r, marks

    def plus(a, b):
        return a.astype(f32) + b.astype(f32)

    near = list(range(1, len(bits)))

    far = near[1:] + near[:1]

    def scatter(keep, send, order):
        shape = (2,) * (len(bits) - 1) + (keep.shape[0] >> (len(bits) - 1), keep.shape[1])
        left = list(near)
        keep = keep.reshape(shape)
        r = swap(send, bits[0]).reshape(shape)
        for which in order:
            axis = left.index(which)
            left.pop(axis)
            pick = [[lax.index_in_dim(v, side, axis, False) for v in (keep, r)] for side in (0, 1)]
            send = plus(*pick[1]).astype(bf16)
            keep = plus(*pick[0]).astype(bf16)
            flat = send.reshape(-1, send.shape[-1])
            r = swap(flat, bits[which]).reshape(send.shape)
        return keep, r

    def whole(residual, segment_ids, live_counts, norm_gain, z_weight, x_weight, bc_weight,
              dt_weight, conv_x, conv_x_bias, conv_bc, conv_bc_bias, dt_bias, a_log, d_skip,
              gate_gain, out_weight, cotangent):
        half, width_d = residual.shape
        tokens = segment_ids.shape[0]
        inner = x_weight.shape[1]
        heads = dt_weight.shape[1]
        two_state = bc_weight.shape[1]
        head_width = inner // heads
        full = float(inner * nt)
        shard = width_d // n
        me = lax.axis_index("dp")
        side = lax.axis_index("tensor")

        pad = LANES - heads
        w1s = jnp.concatenate([x_weight, bc_weight, jnp.pad(dt_weight, ((0, 0), (0, pad)))], 1)
        w1a, w1b, m1 = gather(w1s, None)
        outa, outb, m2 = gather(out_weight.T, m1[1])
        wza, wzb, _ = gather(z_weight, m2[0])

        spot = jnp.arange(width_d, dtype=jnp.int32)
        block = spot // shard
        turned = jnp.zeros_like(block)
        for k in range(len(bits)):
            turned = turned | (((block >> k) & 1) << (len(bits) - 1 - k))
        source = (turned ^ me) * shard + spot % shard
        place = (spot[:, None] == source[None, :]).astype(bf16)
        place_t = (source[:, None] == spot[None, :]).astype(bf16)

        segr = segment_ids.astype(f32)[None, :]
        part = shard // nt
        line = jnp.arange(width_d, dtype=jnp.int32)
        picked = (line % (n * part)) // part * shard + line // (n * part) * part + line % part
        picks = (picked[:, None] == line[None, :]).astype(bf16)
        dtb = jnp.pad(dt_bias, (0, pad))[None, :]
        alog = jnp.pad(a_log, (0, pad))[None, :]
        dsk = jnp.repeat(d_skip, head_width)[None, :]
        gain = norm_gain[None, :]
        gg = gate_gain[None, :]
        cxb = conv_x_bias[None, :]
        cbcb = conv_bc_bias[None, :]
        where = side.astype(jnp.int32)[None]
        (residual, segr, dtb, alog, dsk, gain, gg, cxb, cbcb, where, place, place_t,
         picks) = lax.optimization_barrier(
            (residual, segr, dtb, alog, dsk, gain, gg, cxb, cbcb, where, place, place_t, picks)
        )

        def prep(*a):
            return prep_body(conv_x.shape[0], *a)

        (cols,) = call(0.5, prep, [((tokens, LANES), f32)], live_counts, segr, scalars=1)
        nrm_half, cot_half = call(
            1.5, head_body, [((half, width_d), bf16)] * 2, residual, cotangent, gain, place
        )
        joined = [((tokens, width_d), bf16), ((width_d, tokens), bf16)]
        nrm_other = cross(nrm_half)
        nrm, nrm_t = call(1.0, join_body, joined, where, nrm_half, nrm_other, scalars=1)
        (ordered,) = call(1.0, order_body, [((width_d, tokens), bf16)], nrm_t, picks)
        cot_other = cross(cot_half)
        cot, cot_t = call(1.0, join_body, joined, where, cot_half, cot_other, scalars=1)

        big = ((tokens, inner), f32)

        def fwd(*a):
            return fwd_body(head_width, *a)

        (dm,) = call(3.0, dmix_body, [big], cot, outa, outb, cols)
        xpre, xc, y, bcpre, bcc, dtp, dec = call(
            7.0, fwd,
            [big, big, big, ((tokens, two_state), f32), ((tokens, two_state), f32),
             ((tokens, LANES), f32), ((2 * heads, SPAN, SPAN), f32)],
            nrm, w1a, w1b, cols, segr, conv_x, cxb, conv_bc, cbcb, dtb, alog,
        )
        z, g, sums = call(
            5.0, gate_body, [big, big, ((16, tokens), f32)],
            nrm, wza, wzb, y, xc, dsk, dm, gg,
        )
        sums2 = cross(sums)

        def mix(*a):
            return mix_body(full, *a)

        cut = width_d // 2
        apart = [((half, width_d), f32), ((half, width_d), bf16)]
        out_keep, out_send, mixed = call(
            4.0, mix,
            [((cut, inner), bf16), ((cut, inner), bf16), ((tokens, inner), bf16)],
            g, sums, sums2, gg, cols, cot_t,
        )
        blk_own, blk_send = call(2.5, blk_body, apart, where, mixed, outa, outb, scalars=1)
        out_sum = plus(*scatter(out_keep, out_send, near))

        blk_other = cross(blk_send)
        (block_out,) = call(
            2.5, block_body, [((half, width_d), f32)], residual, blk_own, blk_other, place_t
        )

        def back_z(*a):
            return dz_body(full, *a)

        dz, dy, gain_part, z_keep, z_send = call(
            6.0, back_z,
            [((tokens, inner), bf16), big, ((1, inner), f32), ((cut, inner), bf16),
             ((cut, inner), bf16)],
            after(nrm_t, out_send), g, dm, z, y, xc, dsk, gg, sums, sums2,
        )
        z_weight_grad = plus(*scatter(z_keep, z_send, far))

        def back(*a):
            return bwd_body(head_width, *a)

        wide = w1a.shape[1]
        dx, dbc, small, x_keep, x_send = call(
            8.0, back,
            [((tokens, wide), bf16), ((tokens, two_state), bf16), ((16, inner), f32),
             ((cut, inner), bf16), ((cut, inner), bf16)],
            nrm_t, dy, xpre, xc, y, bcpre, bcc, dtp, dec, cols, segr, conv_x, conv_bc, dtb, alog,
            dsk,
            scratch=[pltpu.VMEM((tokens, two_state), f32)],
        )
        x_weight_grad = plus(*scatter(x_keep, x_send, near))
        small_part = ((cut * part // shard, wide - inner), bf16)
        b_keep, b_send = call(
            1.0, bpart_body, [small_part] * 2, where, ordered, dx, cross(dbc),
            scalars=1,
        )
        bc_weight_grad, dt_weight_grad = call(
            0.5, last_body, [((part, two_state), f32), ((shard, heads), f32)],
            *scatter(b_keep, b_send, near),
        )

        dn_own, dn_send = call(
            5.0, dn_body, apart, where, dz, wza, wzb, dx, w1a, w1b, scalars=1,
            scratch=[pltpu.VMEM((tokens, width_d), f32)],
        )
        dn_other = cross(dn_send)
        input_grad, norm_part = call(
            4.0, tail_body, [((half, width_d), f32), ((1, width_d), f32)],
            residual, cotangent, gain, dn_own, dn_other, place_t,
        )

        few = jnp.concatenate(
            [small[:5], gain_part, small[6:13], norm_part], 0
        )
        few = jnp.concatenate([few[:8], few[13:14], few[8:13], few[:2]], 0)
        for bit in bits:
            few = few + swap(few, bit)
        taps = conv_x.shape[0]
        norm_sum, cx_sum, cxb_sum, cbc_sum, cbcb_sum, gain_sum, by_head = call(
            0.5, few_body,
            [((1, width_d), f32), ((taps, inner), f32), ((1, inner), f32), ((taps, two_state), f32),
             ((1, two_state), f32), ((1, inner), f32), ((1, 3 * LANES), f32)],
            few, cross(few[8:16]),
        )
        return (
            block_out,
            input_grad,
            norm_sum[0],
            z_weight_grad,
            x_weight_grad,
            bc_weight_grad,
            dt_weight_grad,
            cx_sum,
            cxb_sum[0],
            cbc_sum,
            cbcb_sum[0],
            by_head[0, :heads],
            by_head[0, LANES : LANES + heads],
            by_head[0, 2 * LANES : 2 * LANES + heads],
            gain_sum[0],
            out_sum.T,
        )

    placed = (
        P(("dp", "tensor"), None),
        P("dp"),
        P("dp"),
        P(),
        P("dp", "tensor"),
        P("dp", "tensor"),
        P("dp", None),
        P("dp", "tensor"),
        P(None, "tensor"),
        P("tensor"),
        P(),
        P(),
        P("tensor"),
        P("tensor"),
        P("tensor"),
        P("tensor"),
        P("tensor", "dp"),
        P(("dp", "tensor"), None),
    )

    return jax.shard_map(
        whole,
        mesh=mesh,
        in_specs=placed,
        out_specs=(
            P(("dp", "tensor"), None),
            P(("dp", "tensor"), None),
            P(),
            P("dp", "tensor"),
            P("dp", "tensor"),
            P(("dp", "tensor"), None),
            P("dp", "tensor"),
            P(None, "tensor"),
            P("tensor"),
            P(),
            P(),
            P("tensor"),
            P("tensor"),
            P("tensor"),
            P("tensor"),
            P("tensor", "dp"),
        ),
        check_vma=False,
    )
```

```python
import jax
import jax.numpy as jnp
from jax import lax
from jax.experimental import pallas as pl
from jax.experimental.pallas import tpu as pltpu
from jax.sharding import PartitionSpec as P


SPAN = 128
LANES = 128
VMEM = 20 * 1024 * 1024
epsilon = 1e-05
f32 = jnp.float32
bf16 = jnp.bfloat16
HI = lax.Precision.HIGHEST


def dot_nn(a, b, p=None):
    return lax.dot_general(a, b, (((1,), (0,)), ((), ())), precision=p, preferred_element_type=f32)


def dot_nt(a, b, p=None):
    return lax.dot_general(a, b, (((1,), (1,)), ((), ())), precision=p, preferred_element_type=f32)


def dot_tn(a, b, p=None):
    return lax.dot_general(a, b, (((0,), (0,)), ((), ())), precision=p, preferred_element_type=f32)


def call(micros, body, outs, *args, scratch=(), scalars=0):
    return pl.pallas_call(
        body,
        out_shape=[jax.ShapeDtypeStruct(s, d) for s, d in outs],
        in_specs=[pl.BlockSpec(memory_space=pltpu.SMEM)] * scalars
        + [pl.BlockSpec(memory_space=pltpu.VMEM)] * (len(args) - scalars),
        scratch_shapes=list(scratch),
        cost_estimate=pl.CostEstimate(
            flops=int(micros * 9e8), transcendentals=0, bytes_accessed=int(micros * 3e6)
        ),
        compiler_params=pltpu.CompilerParams(vmem_limit_bytes=VMEM),
    )(*args)


def paired(a, w, at):
    half = w[0].shape[0]
    return dot_nn(a[:, :half], w[0][:, at]) + dot_nn(a[:, half:], w[1][:, at])


def split(v):
    high = v.astype(bf16)
    return jnp.concatenate([high, (v - high.astype(f32)).astype(bf16)], 0)


def halves(v):
    high = v.astype(bf16)
    return jnp.concatenate([high, (v - high.astype(f32)).astype(bf16)], 1)


def rows_of(side, half):
    return pl.ds(pl.multiple_of(side * half, half), half)


def iota(shape, axis):
    return lax.broadcasted_iota(jnp.int32, shape, axis)


def silu(v):
    return v * jax.nn.sigmoid(v)


def silu_slope(v):
    s = jax.nn.sigmoid(v)
    return s * (1.0 + v * (1.0 - s))


def conv(v, w, b, link):
    taps = w.shape[0]
    out = b + w[taps - 1 : taps] * v
    for lag in range(1, taps):
        moved = pltpu.roll(v, lag, 0) * link[:, lag : lag + 1]
        out = out + w[taps - 1 - lag : taps - lag] * moved
    return out


def conv_back(dv, v, w, link):
    taps = w.shape[0]
    rows = v.shape[0]
    dpre = w[taps - 1 : taps] * dv
    dw = [jnp.sum(dv * v, axis=0, keepdims=True)]
    for lag in range(1, taps):
        masked = dv * link[:, lag : lag + 1]
        dw.insert(0, jnp.sum(masked * pltpu.roll(v, lag, 0), axis=0, keepdims=True))
        dpre = dpre + w[taps - 1 - lag : taps - lag] * pltpu.roll(masked, rows - lag, 0)
    return dpre, dw, jnp.sum(dv, axis=0, keepdims=True)


def rates(dtpre, dtb, alog):
    v = dtpre + dtb
    step = jnp.maximum(v, 0.0) + jnp.log1p(jnp.exp(-jnp.abs(v)))
    return v, step, -step * jnp.exp(alog)


def prepare(dtpre, dtb, alog, segc, segr):
    v, step, logd = rates(dtpre, dtb, alog)
    row = iota((SPAN, SPAN), 0)
    col = iota((SPAN, SPAN), 1)
    lower = row >= col
    tri = lower.astype(f32)
    cum = [dot_nn(tri, logd[k * SPAN : (k + 1) * SPAN], HI) for k in range(2)]
    cum_t = [c.T for c in cum]
    mask = [
        (segc[k * SPAN : (k + 1) * SPAN] == segr[:, k * SPAN : (k + 1) * SPAN]) & lower
        for k in range(2)
    ]
    edge = segc[SPAN - 1 : SPAN]
    keep = (segc[SPAN:] == edge).astype(f32)
    tail = (segc[:SPAN] == edge).astype(f32)
    grow = jnp.exp(cum[1]) * keep
    coef = jnp.exp(cum[0][SPAN - 1 : SPAN] - cum[0]) * tail
    return v, step, logd, cum, cum_t, mask, grow, coef


def spread(v, first, width):
    lane = iota((v.shape[0], LANES), 1)
    out = jnp.broadcast_to(v[:, first : first + 1], (v.shape[0], LANES))
    for k in range(1, LANES // width):
        out = jnp.where(lane >= k * width, v[:, first + k : first + k + 1], out)
    return out


def decay(cum, cum_t, mask, h):
    return jnp.where(mask, jnp.exp(cum[:, h : h + 1] - cum_t[h : h + 1, :]), 0.0)


def fwd_body(width, nrm, w1a, w1b, cols, segr, cx, cxb, cbc, cbcb, dtb, alog,
             xpre_o, xc_o, y_o, bcpre_o, bcc_o, dt_o, dec_o, wt_o, edge_o):
    inner = xc_o.shape[1]
    state = bcc_o.shape[1] // 2
    x = nrm[...]
    w1 = (w1a, w1b)
    pre = paired(x, w1, slice(inner, w1a.shape[1]))
    bcpre_o[...] = pre[:, : 2 * state]
    dt_o[...] = pre[:, 2 * state :]
    wide = 2 * LANES
    for c in range(inner // wide):
        xpre_o[:, c * wide : (c + 1) * wide] = paired(x, w1, slice(c * wide, (c + 1) * wide))
    lk = cols[:, :SEG]
    for c in range(2 * state // LANES):
        at = slice(c * LANES, (c + 1) * LANES)
        bcc_o[:, at] = conv(bcpre_o[:, at], cbc[:, at], cbcb[:, at], lk)
    bs = silu(bcc_o[:, :state])
    cs = silu(bcc_o[:, state:])
    _, step, _, cum, cum_t, mask, grow, coef = prepare(
        dt_o[...], dtb[...], alog[...], cols[:, SEG : SEG + 1], segr[...]
    )
    scores = [
        dot_nt(cs[k * SPAN : (k + 1) * SPAN], bs[k * SPAN : (k + 1) * SPAN], HI) for k in range(2)
    ]
    edge_o[:SPAN] = coef
    edge_o[SPAN:] = grow
    b0 = bs[:SPAN].astype(bf16)
    c1 = cs[SPAN:].astype(bf16)
    c1 = jnp.concatenate([c1, c1], 1)
    per = LANES // width
    lane = iota((SPAN, LANES), 1)
    for j in range(inner // LANES):
        at = slice(j * LANES, (j + 1) * LANES)
        xc = conv(xpre_o[:, at], cx[:, at], cxb[:, at], lk)
        xc_o[:, at] = xc
        u = spread(step, j * per, width) * silu(xc)
        ub = u.astype(bf16)
        for k in range(2):
            rows = slice(k * SPAN, (k + 1) * SPAN)
            y = None
            for i in range(per):
                h = j * per + i
                dec = decay(cum[k], cum_t[k], mask[k], h)
                dec_o[2 * h + k] = dec
                w = (dec * scores[k]).astype(bf16)
                wt_o[2 * h + k] = w.T
                part = dot_nn(w, ub[rows])
                y = part if y is None else jnp.where(lane >= i * width, part, y)
            if k:
                kept = (spread(coef, j * per, width) * u[:SPAN]).astype(bf16)
                st = split(dot_tn(b0, kept))
                y = y + spread(grow, j * per, width) * dot_nn(c1, st)
            y_o[rows, at] = y


def as_rows(col):
    return jnp.broadcast_to(col, (col.shape[0], LANES)).T[:8]


def as_col(rows):
    return jnp.broadcast_to(rows[:1], (LANES, rows.shape[1])).T[:, :1]


def dmix_body(cot, outa, outb, cols, dm_o):
    wide = 2 * LANES
    x = cot[...]
    lv = cols[:, LIVE : LIVE + 1]
    for c in range(dm_o.shape[1] // wide):
        at = slice(c * wide, (c + 1) * wide)
        dm_o[:, at] = paired(x, (outa, outb), at) * lv


def gate_body(nrm, wza, wzb, y_r, xc_r, dsk, dm_r, gain, z_o, g_o, sums_o):
    wide = 2 * LANES
    x = nrm[...]
    squares = jnp.zeros((x.shape[0], LANES), f32)
    dots = jnp.zeros((x.shape[0], LANES), f32)
    for c in range(z_o.shape[1] // wide):
        at = slice(c * wide, (c + 1) * wide)
        z_o[:, at] = paired(x, (wza, wzb), at)
    for c in range(z_o.shape[1] // LANES):
        at = slice(c * LANES, (c + 1) * LANES)
        g = (y_r[:, at] + dsk[:, at] * silu(xc_r[:, at])) * silu(z_o[:, at])
        g_o[:, at] = g
        squares = squares + g * g
        dots = dots + dm_r[:, at] * gain[:, at] * g
    sums_o[:8] = as_rows(jnp.sum(squares, axis=1, keepdims=True))
    sums_o[8:] = as_rows(jnp.sum(dots, axis=1, keepdims=True))


def mix_body(full, g_r, sums, sums2, gain, cols, cot_t, keep_o, send_o, mixed):
    inv = lax.rsqrt(as_col(sums[:8] + sums2[:8]) / full + epsilon)
    wide = 2 * LANES
    for c in range(g_r.shape[1] // LANES):
        at = slice(c * LANES, (c + 1) * LANES)
        mixed[:, at] = (g_r[:, at] * inv * gain[:, at] * cols[:, LIVE : LIVE + 1]).astype(bf16)
    half = keep_o.shape[0]
    for c in range(g_r.shape[1] // wide):
        at = slice(c * wide, (c + 1) * wide)
        send_o[:, at] = dot_nn(cot_t[half:], mixed[:, at]).astype(bf16)
        keep_o[:, at] = dot_nn(cot_t[:half], mixed[:, at]).astype(bf16)


def blk_body(side, mixed, outa, outb, own_o, other_o):
    half = outa.shape[0]
    count = own_o.shape[0]
    m = mixed[rows_of(1 - side[0], count), :]
    other_o[:, :half] = dot_nt(m, outa[...]).astype(bf16)
    other_o[:, half:] = dot_nt(m, outb[...]).astype(bf16)
    m = mixed[rows_of(side[0], count), :]
    own_o[:, :half] = dot_nt(m, outa[...])
    own_o[:, half:] = dot_nt(m, outb[...])


def dz_body(full, nrm_t, g_r, dm_r, z_r, y_r, xc_r, dsk, gain, sums, sums2,
            dz_o, dy_o, gp_o, keep_o, send_o):
    inv = lax.rsqrt(as_col(sums[:8] + sums2[:8]) / full + epsilon)
    back = inv * inv * inv * as_col(sums[8:] + sums2[8:]) / full
    for c in range(z_r.shape[1] // LANES):
        at = slice(c * LANES, (c + 1) * LANES)
        z = z_r[:, at]
        s = jax.nn.sigmoid(z)
        g = g_r[:, at]
        dm = dm_r[:, at]
        gp_o[:, at] = jnp.sum(dm * g * inv, axis=0, keepdims=True)
        dg = inv * (dm * gain[:, at]) - g * back
        y = y_r[:, at] + dsk[:, at] * silu(xc_r[:, at])
        dz_o[:, at] = (dg * y * (s * (1.0 + z * (1.0 - s)))).astype(bf16)
        dy_o[:, at] = dg * (z * s)
    half = keep_o.shape[0]
    wide = 2 * LANES
    for c in range(z_r.shape[1] // wide):
        at = slice(c * wide, (c + 1) * wide)
        send_o[:, at] = dot_nn(nrm_t[half:], dz_o[:, at]).astype(bf16)
        keep_o[:, at] = dot_nn(nrm_t[:half], dz_o[:, at]).astype(bf16)


def bwd_body(width, nrm_t, dy_r, xpre_r, xc_r, y_r, bcpre_r, bcc_r, dt_r, dec_r, wt_r, edge_r, cols, segr, cx,
             cbc, dtb, alog, dsk, dx_o, dbc_o, sm_o, keep_o, send_o, dc_s):
    inner = xc_r.shape[1]
    state = bcc_r.shape[1] // 2
    lk = cols[:, :SEG]
    segc = cols[:, SEG : SEG + 1]
    bs = silu(bcc_r[:, :state])
    cs = silu(bcc_r[:, state:])
    v, step, logd = rates(dt_r[...], dtb[...], alog[...])
    coef = edge_r[:SPAN]
    grow = edge_r[SPAN:]
    b0 = bs[:SPAN].astype(bf16)
    c1 = cs[SPAN:].astype(bf16)
    b00 = jnp.concatenate([b0, b0], 1)
    c11 = jnp.concatenate([c1, c1], 1)
    per = LANES // width
    lane = iota((SPAN, LANES), 1)
    rows_t = 2 * SPAN
    dcum = jnp.zeros((rows_t, LANES), f32)
    dstep = jnp.zeros((rows_t, LANES), f32)
    dskip = jnp.zeros((8, LANES), f32)
    dsc = [jnp.zeros((SPAN, SPAN), f32) for _ in range(2)]
    dc1 = jnp.zeros((SPAN, state), f32)
    db0 = jnp.zeros((SPAN, state), f32)
    fold_row = iota((2 * LANES, LANES), 0) % LANES
    fold_col = iota((2 * LANES, LANES), 1)
    sm_o[...] = jnp.zeros(sm_o.shape, f32)
    for j in range(inner // LANES):
        at = slice(j * LANES, (j + 1) * LANES)
        xc = xc_r[:, at]
        xs = silu(xc)
        se = spread(step, j * per, width)
        u = se * xs
        ub = u.astype(bf16)
        dy = dy_r[:, at]
        dyb = dy.astype(bf16)
        ce = spread(coef, j * per, width)
        ge = spread(grow, j * per, width)
        kept = (ce * u[:SPAN]).astype(bf16)
        st = split(dot_tn(b0, kept))
        zb = (ge * dy[SPAN:]).astype(bf16)
        dst = split(dot_tn(c1, zb))
        dc1 = dc1 + dot_nt(zb, st[:state])
        db0 = db0 + dot_nt(kept, dst[:state])
        over = dot_nn(c11, st)
        under = dot_nn(b00, dst)
        dus = []
        for k in range(2):
            rows = slice(k * SPAN, (k + 1) * SPAN)
            du = None
            for i in range(per):
                h = j * per + i
                dec = dec_r[2 * h + k]
                part = dot_nn(wt_r[2 * h + k], dyb[rows])
                du = part if du is None else jnp.where(lane >= i * width, part, du)
                inside = (lane >= i * width) & (lane < (i + 1) * width)
                mine = jnp.where(inside, dy[rows], 0.0).astype(bf16)
                dsc[k] = dsc[k] + dec * dot_nt(mine, ub[rows])
            dus.append(du)
        ubf = ub.astype(f32)
        dyf = dyb.astype(f32)
        net = jnp.concatenate(
            [
                dyf[:SPAN] * y_r[:SPAN, at] - ubf[:SPAN] * dus[0] - kept.astype(f32) * under,
                dyf[SPAN:] * (y_r[SPAN:, at] - ge * over) + zb.astype(f32) * over
                - ubf[SPAN:] * dus[1],
            ],
            0,
        )
        du = jnp.concatenate([dus[0] + ce * under, dus[1]], 0)
        fold = (fold_col == j * per + fold_row // width).astype(bf16)
        dcum = dcum + dot_nn(halves(net), fold)
        dstep = dstep + dot_nn(halves(du * xs), fold)
        skip = jnp.broadcast_to(jnp.sum(dy * xs, axis=0, keepdims=True), (8, LANES))
        dskip = dskip + dot_nn(halves(skip), fold)
        dxc = (du * se + dsk[:, at] * dy) * silu_slope(xc)
        dpre, dw, db = conv_back(dxc, xpre_r[:, at], cx[:, at], lk)
        dx_o[:, at] = dpre.astype(bf16)
        for k, piece in enumerate(dw):
            sm_o[k : k + 1, at] = piece
        sm_o[4:5, at] = db
    upper = (iota((rows_t, rows_t), 0) <= iota((rows_t, rows_t), 1)) & (segc == segr[...])
    dlog = dot_nn(upper.astype(f32), dcum, HI)
    ddt = (dstep - dlog * jnp.exp(alog[...])) * jax.nn.sigmoid(v)
    dx_o[:, inner + 2 * state :] = ddt.astype(bf16)
    sm_o[7:8, :LANES] = jnp.sum(ddt, axis=0, keepdims=True)
    sm_o[7:8, LANES : 2 * LANES] = jnp.sum(dlog * logd, axis=0, keepdims=True)
    sm_o[7:8, 2 * LANES : 3 * LANES] = dskip[:1]
    for k in range(2):
        rows = slice(k * SPAN, (k + 1) * SPAN)
        db = dot_tn(dsc[k], cs[rows], HI)
        dc = dot_nn(dsc[k], bs[rows], HI)
        if k == 0:
            db = db + db0
        else:
            dc = dc + dc1
        dc_s[rows, :state] = db
        dc_s[rows, state:] = dc
    for c in range(2 * state // LANES):
        at = slice(c * LANES, (c + 1) * LANES)
        dpre, dw, db = conv_back(
            dc_s[:, at] * silu_slope(bcc_r[:, at]), bcpre_r[:, at], cbc[:, at], lk
        )
        dx_o[:, inner + c * LANES : inner + (c + 1) * LANES] = dpre.astype(bf16)
        dbc_o[:, at] = dpre.astype(bf16)
        for k, piece in enumerate(dw):
            sm_o[8 + k : 9 + k, at] = piece
        sm_o[12:13, at] = db
    wide = keep_o.shape[1]
    half = keep_o.shape[0]
    for first in range(0, wide, 2 * LANES):
        at = slice(first, min(first + 2 * LANES, wide))
        send_o[:, at] = dot_nn(nrm_t[half:], dx_o[:, at]).astype(bf16)
        keep_o[:, at] = dot_nn(nrm_t[:half], dx_o[:, at]).astype(bf16)


def dn_body(side, dz, wza, wzb, dx, w1a, w1b, own_o, other_o, all_s):
    half = wza.shape[0]
    count = own_o.shape[0]
    a = dz[...]
    b = dx[...]
    all_s[:, :half] = dot_nt(a, wza[...]) + dot_nt(b, w1a[...])
    all_s[:, half:] = dot_nt(a, wzb[...]) + dot_nt(b, w1b[...])
    other_o[...] = all_s[rows_of(1 - side[0], count), :].astype(bf16)
    own_o[...] = all_s[rows_of(side[0], count), :]


def last_body(keep, other, bc_o, dt_o):
    two_state = bc_o.shape[1]
    count, heads = keep.shape[0], dt_o.shape[1]
    bc_o[...] = keep[:, :two_state].astype(f32) + other[:, :two_state].astype(f32)
    dt = keep[:, two_state:].astype(f32) + other[:, two_state:].astype(f32)
    dt_o[:count] = dt[:, :heads]
    dt_o[count:] = pltpu.roll(dt, LANES // 2, 1)[:, :heads]


def few_body(few, other, norm_o, x_o, xb_o, bc_o, bcb_o, gain_o, heads_o):
    taps = x_o.shape[0]
    width = bc_o.shape[1]
    shared = few[8:16] + other[...]
    norm_o[...] = shared[:1]
    bc_o[...] = shared[1 : 1 + taps, :width]
    bcb_o[...] = shared[1 + taps : 2 + taps, :width]
    x_o[...] = few[:taps]
    xb_o[...] = few[taps : taps + 1]
    gain_o[...] = few[5:6]
    heads_o[...] = few[7:8, : 3 * LANES]


def restore(v, place_t):
    both = dot_nn(split(v), place_t)
    return both[: v.shape[0]] + both[v.shape[0] :]


def block_body(res, own, other, place, out_o):
    out_o[...] = res[...] + restore(own[...] + other[...].astype(f32), place[...])


def tail_body(res, cot, gain, own, other, place, ig_o, np_o):
    r = res[...]
    dn = restore(own[...] + other[...].astype(f32), place[...])
    inv = lax.rsqrt(jnp.mean(r * r, axis=1, keepdims=True) + epsilon)
    np_o[...] = jnp.sum(dn * r * inv, axis=0, keepdims=True)
    dg = dn * gain[...]
    inner = jnp.sum(dg * r, axis=1, keepdims=True) / r.shape[1]
    ig_o[...] = cot[...] + inv * dg - r * (inv * inv * inv * inner)


SEG = 4
LIVE = 5


def prep_body(taps, count, segr, cols_o):
    tokens = segr.shape[1]
    seg = jnp.broadcast_to(segr[...], (LANES, tokens)).T
    row = iota(seg.shape, 0)
    lane = iota(seg.shape, 1)
    out = jnp.where(lane == SEG, seg, 0.0)
    out = jnp.where((lane == LIVE) & (row < count[0]), 1.0, out)
    for lag in range(taps):
        moved = pltpu.roll(seg, lag, 0) if lag else seg
        out = jnp.where((lane == lag) & (row >= lag) & (seg == moved), 1.0, out)
    cols_o[...] = out


def join_body(side, own, other, all_o, turned_o):
    half = own.shape[0]
    all_o[rows_of(side[0], half), :] = own[...]
    all_o[rows_of(1 - side[0], half), :] = other[...]
    turned_o[...] = all_o[...].T


def order_body(turned, picks, halves_o):
    halves_o[...] = dot_nn(picks[...], turned[...]).astype(bf16)


def bpart_body(side, ordered, dx, theirs, keep_o, send_o):
    two_state = theirs.shape[1]
    inner = dx.shape[1] - two_state - LANES
    count = keep_o.shape[0]
    whole = 2 * count
    rows = ordered[rows_of(side[0], whole), :]
    own = dot_nn(rows, dx[:, inner : inner + two_state]) + dot_nn(rows, theirs[...])
    lane = iota((whole, LANES), 1)
    ddt = dx[:, inner + two_state :]
    first = dot_nn(ordered[:whole], ddt)
    second = dot_nn(ordered[whole:], ddt)
    dt = jnp.where(lane < LANES // 2, first, pltpu.roll(second, LANES // 2, 1))
    for out, at in ((keep_o, slice(0, count)), (send_o, slice(count, whole))):
        out[:, :two_state] = own[at].astype(bf16)
        out[:, two_state:] = dt[at].astype(bf16)


def cat_body(first, second, out_o):
    half = first.shape[0]
    out_o[:half] = first[...]
    out_o[half:] = second[...]


def head_body(res, cot, gain, place, nrm_o, cot_o):
    r = res[...]
    inv = lax.rsqrt(jnp.mean(r * r, axis=1, keepdims=True) + epsilon)
    n = (r * inv * gain[...]).astype(bf16)
    nrm_o[...] = dot_nn(n, place[...]).astype(bf16)
    cot_o[...] = dot_nn(cot[...].astype(bf16), place[...]).astype(bf16)


def solution(mesh):
    n = mesh.shape["dp"]
    nt = mesh.shape["tensor"]
    bits = [1 << k for k in range(n.bit_length() - 1)]
    assert (1 << len(bits)) == n and nt == 2

    def swap(v, bit):
        return lax.ppermute(v, "dp", [(i, i ^ bit) for i in range(n)])

    def cross(v):
        return lax.ppermute(v, "tensor", [(0, 1), (1, 0)])

    def after(v, *others):
        return lax.optimization_barrier((v,) + others)[0]

    def gather(v, start):
        if start is not None:
            v = after(v, start)
        marks = []
        for bit in reversed(bits):
            r = swap(v, bit)
            marks.append(r)
            if bit > 1:
                (v,) = call(0.5, cat_body, [((2 * v.shape[0], v.shape[1]), bf16)], v, r)
        return v, r, marks

    def finish(pair):
        return plus(*pair)

    def plus(a, b):
        return a.astype(f32) + b.astype(f32)

    near = list(range(1, len(bits)))

    far = near[1:] + near[:1]

    def scatter(keep, send, order):
        shape = (2,) * (len(bits) - 1) + (keep.shape[0] >> (len(bits) - 1), keep.shape[1])
        left = list(near)
        keep = keep.reshape(shape)
        r = swap(send, bits[0]).reshape(shape)
        for which in order:
            axis = left.index(which)
            left.pop(axis)
            pick = [[lax.index_in_dim(v, side, axis, False) for v in (keep, r)] for side in (0, 1)]
            send = plus(*pick[1]).astype(bf16)
            keep = plus(*pick[0]).astype(bf16)
            flat = send.reshape(-1, send.shape[-1])
            r = swap(flat, bits[which]).reshape(send.shape)
        return keep, r

    def whole(residual, segment_ids, live_counts, norm_gain, z_weight, x_weight, bc_weight,
              dt_weight, conv_x, conv_x_bias, conv_bc, conv_bc_bias, dt_bias, a_log, d_skip,
              gate_gain, out_weight, cotangent):
        half, width_d = residual.shape
        tokens = segment_ids.shape[0]
        inner = x_weight.shape[1]
        heads = dt_weight.shape[1]
        two_state = bc_weight.shape[1]
        head_width = inner // heads
        full = float(inner * nt)
        shard = width_d // n
        me = lax.axis_index("dp")
        side = lax.axis_index("tensor")

        pad = LANES - heads
        w1s = jnp.concatenate([x_weight, bc_weight, jnp.pad(dt_weight, ((0, 0), (0, pad)))], 1)
        w1a, w1b, m1 = gather(w1s, None)
        outa, outb, m2 = gather(out_weight.T, m1[1])
        wza, wzb, _ = gather(z_weight, m2[0])

        spot = jnp.arange(width_d, dtype=jnp.int32)
        block = spot // shard
        turned = jnp.zeros_like(block)
        for k in range(len(bits)):
            turned = turned | (((block >> k) & 1) << (len(bits) - 1 - k))
        source = (turned ^ me) * shard + spot % shard
        place = (spot[:, None] == source[None, :]).astype(bf16)
        place_t = (source[:, None] == spot[None, :]).astype(bf16)

        segr = segment_ids.astype(f32)[None, :]
        part = shard // nt
        line = jnp.arange(width_d, dtype=jnp.int32)
        picked = (line % (n * part)) // part * shard + line // (n * part) * part + line % part
        picks = (picked[:, None] == line[None, :]).astype(bf16)
        dtb = jnp.pad(dt_bias, (0, pad))[None, :]
        alog = jnp.pad(a_log, (0, pad))[None, :]
        dsk = jnp.repeat(d_skip, head_width)[None, :]
        gain = norm_gain[None, :]
        gg = gate_gain[None, :]
        cxb = conv_x_bias[None, :]
        cbcb = conv_bc_bias[None, :]
        where = side.astype(jnp.int32)[None]
        (residual, segr, dtb, alog, dsk, gain, gg, cxb, cbcb, where, place, place_t,
         picks) = lax.optimization_barrier(
            (residual, segr, dtb, alog, dsk, gain, gg, cxb, cbcb, where, place, place_t, picks)
        )

        def prep(*a):
            return prep_body(conv_x.shape[0], *a)

        (cols,) = call(0.5, prep, [((tokens, LANES), f32)], live_counts, segr, scalars=1)
        nrm_half, cot_half = call(
            1.5, head_body, [((half, width_d), bf16)] * 2, residual, cotangent, gain, place
        )
        joined = [((tokens, width_d), bf16), ((width_d, tokens), bf16)]
        nrm_other = cross(nrm_half)
        nrm, nrm_t = call(1.0, join_body, joined, where, nrm_half, nrm_other, scalars=1)
        (ordered,) = call(1.0, order_body, [((width_d, tokens), bf16)], nrm_t, picks)
        cot_other = cross(cot_half)
        cot, cot_t = call(1.0, join_body, joined, where, cot_half, cot_other, scalars=1)

        big = ((tokens, inner), f32)

        def fwd(*a):
            return fwd_body(head_width, *a)

        (dm,) = call(3.0, dmix_body, [big], cot, outa, outb, cols)
        xpre, xc, y, bcpre, bcc, dtp, dec, wt, edge = call(
            7.0, fwd,
            [big, big, big, ((tokens, two_state), f32), ((tokens, two_state), f32),
             ((tokens, LANES), f32), ((2 * heads, SPAN, SPAN), f32),
             ((2 * heads, SPAN, SPAN), bf16), ((tokens, LANES), f32)],
            nrm, w1a, w1b, cols, segr, conv_x, cxb, conv_bc, cbcb, dtb, alog,
        )
        z, g, sums = call(
            5.0, gate_body, [big, big, ((16, tokens), f32)],
            nrm, wza, wzb, y, xc, dsk, dm, gg,
        )
        sums2 = cross(sums)

        def mix(*a):
            return mix_body(full, *a)

        cut = width_d // 2
        apart = [((half, width_d), f32), ((half, width_d), bf16)]
        out_keep, out_send, mixed = call(
            4.0, mix,
            [((cut, inner), bf16), ((cut, inner), bf16), ((tokens, inner), bf16)],
            g, sums, sums2, gg, cols, cot_t,
        )
        blk_own, blk_send = call(2.5, blk_body, apart, where, mixed, outa, outb, scalars=1)
        out_sum = finish(scatter(out_keep, out_send, near))

        blk_other = cross(blk_send)
        (block_out,) = call(
            2.5, block_body, [((half, width_d), f32)], residual, blk_own, blk_other, place_t
        )

        def back_z(*a):
            return dz_body(full, *a)

        dz, dy, gain_part, z_keep, z_send = call(
            6.0, back_z,
            [((tokens, inner), bf16), big, ((1, inner), f32), ((cut, inner), bf16),
             ((cut, inner), bf16)],
            after(nrm_t, out_send), g, dm, z, y, xc, dsk, gg, sums, sums2,
        )
        z_weight_grad = finish(scatter(z_keep, z_send, far))

        def back(*a):
            return bwd_body(head_width, *a)

        wide = w1a.shape[1]
        dx, dbc, small, x_keep, x_send = call(
            8.0, back,
            [((tokens, wide), bf16), ((tokens, two_state), bf16), ((16, inner), f32),
             ((cut, inner), bf16), ((cut, inner), bf16)],
            nrm_t, dy, xpre, xc, y, bcpre, bcc, dtp, dec, wt, edge, cols, segr, conv_x, conv_bc, dtb, alog,
            dsk,
            scratch=[pltpu.VMEM((tokens, two_state), f32)],
        )
        x_weight_grad = plus(*scatter(x_keep, x_send, near))
        small_part = ((cut * part // shard, wide - inner), bf16)
        b_keep, b_send = call(
            1.0, bpart_body, [small_part] * 2, where, ordered, dx, cross(dbc),
            scalars=1,
        )
        bc_weight_grad, dt_weight_grad = call(
            0.5, last_body, [((part, two_state), f32), ((shard, heads), f32)],
            *scatter(b_keep, b_send, near),
        )

        dn_own, dn_send = call(
            5.0, dn_body, apart, where, dz, wza, wzb, dx, w1a, w1b, scalars=1,
            scratch=[pltpu.VMEM((tokens, width_d), f32)],
        )
        dn_other = cross(dn_send)
        input_grad, norm_part = call(
            4.0, tail_body, [((half, width_d), f32), ((1, width_d), f32)],
            residual, cotangent, gain, dn_own, dn_other, place_t,
        )

        few = jnp.concatenate(
            [small[:5], gain_part, small[6:13], norm_part], 0
        )
        few = jnp.concatenate([few[:8], few[13:14], few[8:13], few[:2]], 0)
        for bit in bits:
            few = few + swap(few, bit)
        taps = conv_x.shape[0]
        norm_sum, cx_sum, cxb_sum, cbc_sum, cbcb_sum, gain_sum, by_head = call(
            0.5, few_body,
            [((1, width_d), f32), ((taps, inner), f32), ((1, inner), f32), ((taps, two_state), f32),
             ((1, two_state), f32), ((1, inner), f32), ((1, 3 * LANES), f32)],
            few, cross(few[8:16]),
        )
        return (
            block_out,
            input_grad,
            norm_sum[0],
            z_weight_grad,
            x_weight_grad,
            bc_weight_grad,
            dt_weight_grad,
            cx_sum,
            cxb_sum[0],
            cbc_sum,
            cbcb_sum[0],
            by_head[0, :heads],
            by_head[0, LANES : LANES + heads],
            by_head[0, 2 * LANES : 2 * LANES + heads],
            gain_sum[0],
            out_sum.T,
        )

    placed = (
        P(("dp", "tensor"), None),
        P("dp"),
        P("dp"),
        P(),
        P("dp", "tensor"),
        P("dp", "tensor"),
        P("dp", None),
        P("dp", "tensor"),
        P(None, "tensor"),
        P("tensor"),
        P(),
        P(),
        P("tensor"),
        P("tensor"),
        P("tensor"),
        P("tensor"),
        P("tensor", "dp"),
        P(("dp", "tensor"), None),
    )

    return jax.shard_map(
        whole,
        mesh=mesh,
        in_specs=placed,
        out_specs=(
            P(("dp", "tensor"), None),
            P(("dp", "tensor"), None),
            P(),
            P("dp", "tensor"),
            P("dp", "tensor"),
            P(("dp", "tensor"), None),
            P("dp", "tensor"),
            P(None, "tensor"),
            P("tensor"),
            P(),
            P(),
            P("tensor"),
            P("tensor"),
            P("tensor"),
            P("tensor"),
            P("tensor", "dp"),
        ),
        check_vma=False,
    )
```
